512 devices in a mesh: dp: 32 (over z, x_lo), fsdp: 16 (over y, x_hi, core).
Axes of the slice: x: 4 (x_hi: 2, x_lo: 2; x = x_hi * 2 + x_lo), y: 4, z: 16, core: 2. Of those that a mesh axis runs over, the one named last changes fastest.
Arguments:
- images: bfloat16 [1024, 8, 8, 3072], P(('dp', 'fsdp')), may hold values from -6 to 6
- dw_weight: float32 [49, 3072], P(None, 'fsdp'), may hold values from -0.875 to 0.875
- dw_bias: float32 [3072], P('fsdp'), may hold values from -1 to 1
- block_gain: float32 [3072], P('fsdp'), may hold values from 0.5 to 1.5
- head_gain: float32 [3072], P('fsdp'), may hold values from 0.5 to 1.5
- projection: bfloat16 [3072, 512], P('fsdp'), may hold values from -0.109375 to 0.109375
- text: bfloat16 [1024, 512], P(('dp', 'fsdp')), may hold values from -6 to 6
Outputs:
- loss: float32 [], replicated
- grad_images: bfloat16 [1024, 8, 8, 3072], P(('dp', 'fsdp'))
- grad_dw_weight: float32 [49, 3072], P(None, 'fsdp')
- grad_dw_bias: float32 [3072], P('fsdp')
- grad_block_gain: float32 [3072], P('fsdp')
- grad_head_gain: float32 [3072], P('fsdp')
- grad_projection: float32 [3072, 512], P('fsdp')
- grad_text: float32 [1024, 512], P(('dp', 'fsdp'))
The draws below stay inside these ranges and needn't reach their ends.
All inputs are finite; a program needn't handle non-finite values.
Results may differ from the reference program's by a relative error of at most 0.012.
Values may be sent and summed in bfloat16 or wider, within the bound.
A program may use at most 64 MiB of HBM per device.

```python
import jax
import jax.numpy as jnp
from jax import lax

CHANNELS = 3072
EMBED = 512
KERNEL = 7
MAP_SIDE = 8
IMG_DEV = 2
BATCH = 1024
N_DP = 32
N_FSDP = 16


def shard_levels(stream_key, dims, cuts, low, largest):
    factor_of = 1.0
    for dim, parts in cuts:
        steps = jax.random.uniform(jax.random.fold_in(jax.random.fold_in(stream_key, 6), dim), (parts,), jnp.float32, low / len(cuts), largest / len(cuts))
        factor_of = factor_of * jnp.repeat(jnp.exp(steps), dims[dim] // parts).reshape((-1,) + (1,) * (len(dims) - 1 - dim))
    return factor_of


def bell_draw(key, extent, scale, limit, cuts=(), kind=jnp.bfloat16):
    factor_of = shard_levels(key, extent, cuts, -0.22, 0.18) if cuts else 1.0
    array = jax.random.normal(key, extent, jnp.float32) * scale * factor_of
    return jnp.minimum(jnp.maximum(array, -limit), limit).astype(kind)


def setup_inputs(seed: int = 0) -> dict:
    splits = jax.random.split(jax.random.key(seed), 8)
    return {
        "images": bell_draw(splits[0], (BATCH, MAP_SIDE, MAP_SIDE, CHANNELS), 1.0, 6.0, ((0, 512),)),
        "dw_weight": bell_draw(splits[1], (KERNEL * KERNEL, CHANNELS), (KERNEL * KERNEL) ** -0.5, 0.875, ((1, 16),), jnp.float32),
        "dw_bias": jnp.clip(jax.random.uniform(splits[2], (CHANNELS,), jnp.float32, -1.0, 1.0) * shard_levels(splits[2], (CHANNELS,), ((0, 16),), -0.4, 0.0), -1.0, 1.0),
        "block_gain": jnp.clip(0.5 + 1.0 * jax.random.uniform(splits[3], (CHANNELS,), jnp.float32) ** shard_levels(splits[3], (CHANNELS,), ((0, 16),), -0.2, 0.2), 0.5, 1.5),
        "head_gain": jnp.clip(0.5 + 1.0 * jax.random.uniform(splits[4], (CHANNELS,), jnp.float32) ** shard_levels(splits[4], (CHANNELS,), ((0, 16),), -0.2, 0.2), 0.5, 1.5),
        "projection": bell_draw(splits[5], (CHANNELS, EMBED), CHANNELS ** -0.5, 0.109375, ((0, 16),)),
        "text": bell_draw(splits[6], (BATCH, EMBED), 1.0, 6.0, ((0, 512),)),
    }


LOGIT_SCALE = 14.0
EPSILON = 1e-06

def depthwise(padded, weight):
    total = jnp.zeros(padded.shape[:1] + (MAP_SIDE, MAP_SIDE, padded.shape[3]), jnp.float32)
    for tap_row in range(KERNEL):
        for tap_col in range(KERNEL):
            window = padded[:, tap_row:tap_row + MAP_SIDE, tap_col:tap_col + MAP_SIDE, :]
            total = total + window * weight[tap_row * KERNEL + tap_col]
    return total

def tower_forward(images, dw_weight, dw_bias, block_gain, head_gain):
    margin = KERNEL // 2
    as_float = images.astype(jnp.float32)
    padded = jnp.pad(as_float, ((0, 0), (margin, margin), (margin, margin), (0, 0)))
    conv_out = depthwise(padded, dw_weight) + dw_bias
    centred = conv_out - lax.optimization_barrier(jnp.mean(conv_out, axis=3, keepdims=True))
    inverse = lax.rsqrt(lax.optimization_barrier(jnp.mean(centred * centred, axis=3, keepdims=True)) + EPSILON)
    normal_z = centred * inverse
    hidden = as_float + normal_z * block_gain
    pooled = lax.optimization_barrier(jnp.mean(hidden, axis=(1, 2)))
    pool_centred = pooled - lax.optimization_barrier(jnp.mean(pooled, axis=1, keepdims=True))
    pool_inverse = lax.rsqrt(lax.optimization_barrier(jnp.mean(pool_centred * pool_centred, axis=1, keepdims=True)) + EPSILON)
    pool_normed = pool_centred * pool_inverse
    query = (pool_normed * head_gain).astype(jnp.bfloat16)
    return (padded, normal_z, inverse, pool_normed, pool_inverse, query)

def tower_backward(padded, normal_z, inverse, pool_normed, pool_inverse, d_query, dw_weight, block_gain, head_gain):
    d_normed = d_query * head_gain
    g_head = lax.optimization_barrier(jnp.sum(d_query * pool_normed, axis=0))
    d_pooled = pool_inverse * (d_normed - lax.optimization_barrier(jnp.mean(d_normed, axis=1, keepdims=True)) - pool_normed * lax.optimization_barrier(jnp.mean(d_normed * pool_normed, axis=1, keepdims=True)))
    d_hidden = (d_pooled / float(MAP_SIDE * MAP_SIDE))[:, None, None, :]
    d_norm = d_hidden * block_gain
    g_block = lax.optimization_barrier(jnp.sum(d_hidden * normal_z, axis=(0, 1, 2)))
    d_conv = inverse * (d_norm - lax.optimization_barrier(jnp.mean(d_norm, axis=3, keepdims=True)) - normal_z * lax.optimization_barrier(jnp.mean(d_norm * normal_z, axis=3, keepdims=True)))
    g_bias = lax.optimization_barrier(jnp.sum(d_conv, axis=(0, 1, 2)))
    margin = KERNEL // 2
    d_padded = jnp.pad(d_conv, ((0, 0), (margin, margin), (margin, margin), (0, 0)))
    tap_grads = []
    d_images = d_hidden + jnp.zeros_like(d_conv)
    for tap_row in range(KERNEL):
        for tap_col in range(KERNEL):
            window = padded[:, tap_row:tap_row + MAP_SIDE, tap_col:tap_col + MAP_SIDE, :]
            tap_grads.append(lax.optimization_barrier(jnp.sum(d_conv * window, axis=(0, 1, 2))))
            back = d_padded[:, 2 * margin - tap_row:2 * margin - tap_row + MAP_SIDE, 2 * margin - tap_col:2 * margin - tap_col + MAP_SIDE, :]
            d_images = d_images + back * dw_weight[tap_row * KERNEL + tap_col]
    return (d_images.astype(jnp.bfloat16), jnp.stack(tap_grads), g_bias, g_block, g_head)

def reference(images, dw_weight, dw_bias, block_gain, head_gain, projection, text):
    groups = N_DP * N_FSDP
    blocks = images.reshape((groups, IMG_DEV, MAP_SIDE, MAP_SIDE, CHANNELS))

    def forward_block(block):
        return tower_forward(block, dw_weight, dw_bias, block_gain, head_gain)[5]
    queries = lax.map(forward_block, blocks).reshape((BATCH, CHANNELS))
    embedding = jnp.dot(queries, projection, preferred_element_type=jnp.float32)
    image_scale = lax.rsqrt(lax.optimization_barrier(jnp.sum(embedding * embedding, axis=1, keepdims=True)) + EPSILON)
    image_f = embedding * image_scale
    image_unit = image_f.astype(jnp.bfloat16)
    text_float = text.astype(jnp.float32)
    text_scale = lax.rsqrt(lax.optimization_barrier(jnp.sum(text_float * text_float, axis=1, keepdims=True)) + EPSILON)
    text_f = text_float * text_scale
    text_unit = text_f.astype(jnp.bfloat16)
    logits = LOGIT_SCALE * jnp.dot(image_unit, text_unit.T, preferred_element_type=jnp.float32)
    row_lse = jnp.log(lax.optimization_barrier(jnp.sum(jnp.exp(logits), axis=1)))
    col_lse = jnp.log(lax.optimization_barrier(jnp.sum(jnp.exp(logits), axis=0)))
    diagonal = LOGIT_SCALE * lax.optimization_barrier(jnp.sum(image_unit.astype(jnp.float32) * text_unit.astype(jnp.float32), axis=1))
    loss = (jnp.sum(row_lse) + jnp.sum(col_lse) - 2.0 * jnp.sum(diagonal)) / (2.0 * BATCH)
    identity = jnp.eye(BATCH, dtype=jnp.float32)
    weights = (jnp.exp(logits - row_lse[:, None]) + jnp.exp(logits - col_lse[None, :]) - 2.0 * identity).astype(jnp.bfloat16)
    d_image = 7.0 * jnp.dot(weights, text_unit, preferred_element_type=jnp.float32)
    d_caption = 7.0 * jnp.dot(weights.T, image_unit, preferred_element_type=jnp.float32)
    d_embedding = (image_scale * (d_image - image_f * lax.optimization_barrier(jnp.sum(image_f * d_image, axis=1, keepdims=True)))).astype(jnp.bfloat16)
    grad_text = text_scale * (d_caption - text_f * lax.optimization_barrier(jnp.sum(text_f * d_caption, axis=1, keepdims=True)))
    grad_projection = jnp.dot(queries.T, d_embedding, preferred_element_type=jnp.float32)
    d_query = jnp.dot(d_embedding, projection.T, preferred_element_type=jnp.float32)
    d_blocks = d_query.reshape((groups, IMG_DEV, CHANNELS))

    def backward_block(carry, inputs):
        block, d_block = inputs
        padded, normal_z, inverse, pool_normed, pool_inverse, query = tower_forward(block, dw_weight, dw_bias, block_gain, head_gain)
        d_images, g_weight, g_bias, g_block, g_head = tower_backward(padded, normal_z, inverse, pool_normed, pool_inverse, d_block, dw_weight, block_gain, head_gain)
        return ((carry[0] + g_weight, carry[1] + g_bias, carry[2] + g_block, carry[3] + g_head), d_images)
    zeros_c = jnp.zeros((CHANNELS,), jnp.float32)
    init = (jnp.zeros((KERNEL * KERNEL, CHANNELS), jnp.float32), zeros_c, zeros_c, zeros_c)
    sums, d_maps = lax.scan(backward_block, init, (blocks, d_blocks))
    grad_images = d_maps.reshape(images.shape)
    return (loss, grad_images, sums[0], sums[1], sums[2], sums[3], grad_projection, grad_text)
```

```python
import jax
import jax.numpy as jnp
from jax import lax
from jax.sharding import PartitionSpec as P

KERNEL = 7
MAP_SIDE = 8


LOGIT_SCALE = 14.0
EPSILON = 1e-06


def depthwise(padded, weight):
    total = jnp.zeros(padded.shape[:1] + (MAP_SIDE, MAP_SIDE, padded.shape[3]), jnp.float32)
    for tap_row in range(KERNEL):
        for tap_col in range(KERNEL):
            window = padded[:, tap_row : tap_row + MAP_SIDE, tap_col : tap_col + MAP_SIDE, :]
            total = total + window * weight[tap_row * KERNEL + tap_col]
    return total


def contract(left, right, left_dim, right_dim):
    return lax.dot_general(
        left, right, (((left_dim,), (right_dim,)), ((), ())), preferred_element_type=jnp.float32
    )


N_DP = 32
N_FSDP = 16


def share(value, axis, count):
    return lax.all_to_all(
        jnp.broadcast_to(value[None], (count,) + value.shape), axis, split_axis=0, concat_axis=0, tiled=True
    )


def swap(blocks, axis):
    return lax.all_to_all(blocks, axis, split_axis=0, concat_axis=0, tiled=True)


def local(images, dw_weight, dw_bias, block_gain, head_gain, projection, text):
    channels = images.shape[3]
    shard = dw_bias.shape[0]
    count = images.shape[0]
    embed = text.shape[1]
    pack = jnp.concatenate([dw_weight, dw_bias[None], block_gain[None]], axis=0)
    pack_all = share(pack, "fsdp", N_FSDP).transpose(1, 0, 2).reshape(pack.shape[0], channels)
    full_weight, full_bias, full_block = pack_all[:49], pack_all[49], pack_all[50]
    text_float = text.astype(jnp.float32)
    text_scale = lax.rsqrt(jnp.sum(text_float * text_float, axis=1, keepdims=True) + EPSILON)
    text_f = text_float * text_scale
    text_unit = text_f.astype(jnp.bfloat16)
    text_cols = share(text_unit, "dp", N_DP).reshape(N_DP * count, embed)

    margin = KERNEL // 2
    as_float = images.astype(jnp.float32)
    padded = jnp.pad(as_float, ((0, 0), (margin, margin), (margin, margin), (0, 0)))
    conv_out = depthwise(padded, full_weight) + full_bias
    centred = conv_out - jnp.mean(conv_out, axis=3, keepdims=True)
    inverse = lax.rsqrt(jnp.mean(centred * centred, axis=3, keepdims=True) + EPSILON)
    normal_z = centred * inverse
    hidden = as_float + normal_z * full_block
    pooled = jnp.mean(hidden, axis=(1, 2))
    pool_centred = pooled - jnp.mean(pooled, axis=1, keepdims=True)
    pool_inverse = lax.rsqrt(jnp.mean(pool_centred * pool_centred, axis=1, keepdims=True) + EPSILON)
    pool_normed = pool_centred * pool_inverse

    normed_group = swap(
        pool_normed.reshape(count, N_FSDP, shard).transpose(1, 0, 2), "fsdp"
    ).reshape(N_FSDP * count, shard)
    query_group = (normed_group * head_gain).astype(jnp.bfloat16)
    part = jnp.dot(query_group, projection, preferred_element_type=jnp.float32)
    embedding = jnp.sum(swap(part.reshape(N_FSDP, count, embed), "fsdp"), axis=0)
    image_scale = lax.rsqrt(jnp.sum(embedding * embedding, axis=1, keepdims=True) + EPSILON)
    image_f = embedding * image_scale
    image_unit = image_f.astype(jnp.bfloat16)
    image_rows = share(image_unit, "fsdp", N_FSDP).reshape(N_FSDP * count, embed)

    logits = LOGIT_SCALE * contract(image_rows, text_cols, 1, 1)
    exps = jnp.exp(logits)
    row_lse = jnp.log(jnp.sum(share(jnp.sum(exps, axis=1), "fsdp", N_FSDP), axis=0))
    col_lse = jnp.log(jnp.sum(share(jnp.sum(exps, axis=0), "dp", N_DP), axis=0))
    group = lax.axis_index("dp")
    member = lax.axis_index("fsdp")
    rows = jnp.arange(N_FSDP * count, dtype=jnp.int32)[:, None]
    cols = jnp.arange(N_DP * count, dtype=jnp.int32)[None, :]
    same = (
        (rows // count == member) & (cols // count == group) & (rows % count == cols % count)
    ).astype(jnp.float32)
    diagonal = LOGIT_SCALE * jnp.sum(
        image_unit.astype(jnp.float32) * text_unit.astype(jnp.float32), axis=1
    )
    loss_part = (
        jnp.sum(row_lse) / N_FSDP + jnp.sum(col_lse) / N_DP - 2.0 * jnp.sum(diagonal)
    )
    weights = (
        jnp.exp(logits - row_lse[:, None]) + jnp.exp(logits - col_lse[None, :]) - 2.0 * same
    ).astype(jnp.bfloat16)
    d_image = 7.0 * jnp.sum(
        swap(
            jnp.dot(weights, text_cols, preferred_element_type=jnp.float32).reshape(
                N_FSDP, count, embed
            ),
            "fsdp",
        ),
        axis=0,
    )
    d_embedding = (
        image_scale * (d_image - image_f * jnp.sum(image_f * d_image, axis=1, keepdims=True))
    ).astype(jnp.bfloat16)
    d_caption = 7.0 * jnp.sum(
        swap(contract(weights, image_rows, 0, 0).reshape(N_DP, count, embed), "dp"), axis=0
    )
    grad_text = text_scale * (
        d_caption - text_f * jnp.sum(text_f * d_caption, axis=1, keepdims=True)
    )
    demb_group = share(d_embedding, "fsdp", N_FSDP).reshape(N_FSDP * count, embed)
    proj_grad = contract(query_group, demb_group, 0, 0)
    d_query = contract(demb_group, projection, 1, 1)
    g_head = jnp.sum(d_query * normed_group, axis=0)
    d_normed = (
        swap((d_query * head_gain).reshape(N_FSDP, count, shard), "fsdp")
        .transpose(1, 0, 2)
        .reshape(count, channels)
    )
    d_pooled = pool_inverse * (
        d_normed
        - jnp.mean(d_normed, axis=1, keepdims=True)
        - pool_normed * jnp.mean(d_normed * pool_normed, axis=1, keepdims=True)
    )
    d_hidden = (d_pooled / float(MAP_SIDE * MAP_SIDE))[:, None, None, :]
    d_norm = d_hidden * full_block
    g_block = jnp.sum(d_hidden * normal_z, axis=(0, 1, 2))
    d_conv = inverse * (
        d_norm
        - jnp.mean(d_norm, axis=3, keepdims=True)
        - normal_z * jnp.mean(d_norm * normal_z, axis=3, keepdims=True)
    )
    g_bias = jnp.sum(d_conv, axis=(0, 1, 2))
    d_padded = jnp.pad(d_conv, ((0, 0), (margin, margin), (margin, margin), (0, 0)))
    tap_grads = []
    d_images = d_hidden + jnp.zeros_like(d_conv)
    for tap_row in range(KERNEL):
        for tap_col in range(KERNEL):
            window = padded[:, tap_row : tap_row + MAP_SIDE, tap_col : tap_col + MAP_SIDE, :]
            tap_grads.append(jnp.sum(d_conv * window, axis=(0, 1, 2)))
            back = d_padded[
                :,
                2 * margin - tap_row : 2 * margin - tap_row + MAP_SIDE,
                2 * margin - tap_col : 2 * margin - tap_col + MAP_SIDE,
                :,
            ]
            d_images = d_images + back * full_weight[tap_row * KERNEL + tap_col]
    grads = jnp.stack(tap_grads + [g_bias, g_block, jnp.full((channels,), loss_part)])
    held = jnp.sum(
        swap(grads.reshape(52, N_FSDP, shard).transpose(1, 0, 2), "fsdp"), axis=0
    )
    small = jnp.concatenate([held, g_head[None], jnp.zeros((11, shard), jnp.float32)])
    both = jnp.concatenate(
        [small.reshape(N_DP, 2 * shard), proj_grad.reshape(N_DP, shard // N_DP * embed)], axis=1
    )
    total = share(jnp.sum(swap(both[:, None], "dp"), axis=0), "dp", N_DP).reshape(both.shape)
    sums = total[:, : 2 * shard].reshape(64, shard)
    sum_proj = total[:, 2 * shard :].reshape(shard, embed)
    pairs = N_DP * N_FSDP * count
    return (
        sums[51, 0] / (2.0 * pairs),
        d_images.astype(jnp.bfloat16),
        sums[:49],
        sums[49],
        sums[50],
        sums[52],
        sum_proj,
        grad_text,
    )


def solution(mesh):
    return jax.shard_map(
        local,
        mesh=mesh,
        in_specs=(
            P(("dp", "fsdp"), None, None, None),
            P(None, "fsdp"),
            P("fsdp"),
            P("fsdp"),
            P("fsdp"),
            P("fsdp", None),
            P(("dp", "fsdp"), None),
        ),
        out_specs=(
            P(),
            P(("dp", "fsdp"), None, None, None),
            P(None, "fsdp"),
            P("fsdp"),
            P("fsdp"),
            P("fsdp"),
            P("fsdp", None),
            P(("dp", "fsdp"), None),
        ),
        check_vma=False,
    )
```

```python
import jax
import jax.numpy as jnp
from jax import lax
from jax.experimental import pallas as pl
from jax.experimental.pallas import tpu as pltpu
from jax.sharding import PartitionSpec as P

KERNEL = 7
MAP_SIDE = 8
LOGIT_SCALE = 14.0
EPSILON = 1e-06
MESH = pl.DeviceIdType.MESH
F32 = jnp.float32
BF16 = jnp.bfloat16
N_DP = 32
N_FSDP = 16
IMGS = 2
CHANNELS = 3072
SHARD = 192
EMBED = 512
ROWS = 56
BIAS_ROW, BLOCK_ROW, HEAD_ROW, LOSS_ROW = 49, 50, 51, 52
BLOCKS = CHANNELS // 128
VMEM_SPEC = pl.BlockSpec(memory_space=pltpu.VMEM)


def contract(left, right, left_dim, right_dim):
    return lax.dot_general(
        left, right, (((left_dim,), (right_dim,)), ((), ())), preferred_element_type=F32
    )


def copy_to(axis, peer, src, dst, send_sem, recv_sem):
    return pltpu.make_async_remote_copy(
        src_ref=src,
        dst_ref=dst,
        send_sem=send_sem,
        recv_sem=recv_sem,
        device_id={axis: peer},
        device_id_type=MESH,
    )


def loop(low, high, body):
    def step(t, carry):
        body(t)
        return carry

    lax.fori_loop(low, high, step, 0)


def greet(me_f, me_d, with_dp):
    barrier = pltpu.get_barrier_semaphore()

    def signal(axis, me, count):
        def body(t):
            peer = lax.rem(me + t, count)
            pl.semaphore_signal(barrier, inc=1, device_id={axis: peer}, device_id_type=MESH)

        loop(1, count, body)

    total = N_FSDP - 1
    if with_dp:
        signal("dp", me_d, N_DP)
        total += N_DP - 1
    signal("fsdp", me_f, N_FSDP)
    pl.semaphore_wait(barrier, total)


class Exchange:
    def __init__(self, axis, count, me, source, dst, send_sem, recv_sem):
        self.axis, self.count, self.me = axis, count, me
        self.source, self.dst, self.send_sem, self.recv_sem = source, dst, send_sem, recv_sem

    def _each(self, act):
        def body(t):
            act(t, lax.rem(self.me + t, self.count))

        loop(1, self.count, body)

    def start(self):
        def act(t, peer):
            copy_to(
                self.axis, peer, self.source(peer), self.dst.at[self.me],
                self.send_sem.at[t], self.recv_sem.at[self.me],
            ).start()

        self._each(act)

    def wait_recv(self):
        def act(t, peer):
            copy_to(
                self.axis, peer, self.source(peer), self.dst.at[peer],
                self.send_sem.at[t], self.recv_sem.at[peer],
            ).wait_recv()

        self._each(act)

    def wait_send(self):
        def act(t, peer):
            copy_to(
                self.axis, peer, self.source(peer), self.dst.at[self.me],
                self.send_sem.at[t], self.recv_sem.at[self.me],
            ).wait_send()

        self._each(act)


def join_pairs(read, write):
    for p in range(N_FSDP // 2):
        write(p, jnp.concatenate([read(2 * p), read(2 * p + 1)], axis=1))


def shifted(value, amount):
    if amount == 0:
        return value
    place = lax.broadcasted_iota(jnp.int32, value.shape, 0)
    rolled = pltpu.roll(value, amount % MAP_SIDE, 0)
    inside = place >= amount if amount > 0 else place < MAP_SIDE + amount
    return jnp.where(inside, rolled, 0.0)


def lanes_of(block):
    return pl.ds(pl.multiple_of(block * 128, 128), 128)


def gather_kernel(w_ref, bias_ref, gain_ref, full_ref, pack, held, send_sem, recv_sem):
    me_f, me_d = lax.axis_index("fsdp"), lax.axis_index("dp")
    rows = jnp.concatenate(
        [w_ref[...], bias_ref[...], gain_ref[...], jnp.zeros((ROWS - 51, SHARD), F32)], axis=0
    )
    pack[...] = rows
    held[me_f] = rows
    greet(me_f, me_d, False)
    ex = Exchange("fsdp", N_FSDP, me_f, lambda peer: pack, held, send_sem, recv_sem)
    ex.start()
    ex.wait_recv()

    def write(p, value):
        full_ref[:, 384 * p : 384 * (p + 1)] = value

    join_pairs(lambda s: held[s], write)
    ex.wait_send()


def forward_kernel(images, full, z_ref, inv_ref, zsum_ref, normed_ref, poolinv_ref, sums, isum, pooled):
    margin = KERNEL // 2
    sums[...] = jnp.zeros_like(sums)

    def conv(block):
        lanes = lanes_of(block)
        for b in range(IMGS):
            rows = [images[b, i, :, lanes].astype(F32) for i in range(MAP_SIDE)]
            total = rows[0]
            for i in range(1, MAP_SIDE):
                total = total + rows[i]
            isum[b, :, lanes] = total
            bias = jnp.broadcast_to(full[pl.ds(BIAS_ROW, 1), lanes], (MAP_SIDE, 128))
            acc = [bias] * MAP_SIDE
            for s in range(KERNEL):
                cols = [shifted(row, margin - s) for row in rows]
                for r in range(KERNEL):
                    tap = jnp.broadcast_to(
                        full[pl.ds(r * KERNEL + s, 1), lanes], (MAP_SIDE, 128)
                    )
                    for i in range(MAP_SIDE):
                        if 0 <= i + r - margin < MAP_SIDE:
                            acc[i] = acc[i] + cols[i + r - margin] * tap
            for i in range(MAP_SIDE):
                z_ref[b, i, :, lanes] = acc[i]
                sums[b, i] += acc[i]

    loop(0, BLOCKS, conv)
    mean = jnp.sum(sums[...], axis=3, keepdims=True) * (1.0 / CHANNELS)
    mean = jnp.broadcast_to(mean, sums.shape)
    inv_ref[...] = mean
    sums[...] = jnp.zeros_like(sums)

    def centre(block):
        lanes = lanes_of(block)
        value = z_ref[:, :, :, lanes] - inv_ref[...]
        z_ref[:, :, :, lanes] = value
        sums[...] += value * value

    loop(0, BLOCKS, centre)
    var = jnp.sum(sums[...], axis=3, keepdims=True) * (1.0 / CHANNELS)
    inv_ref[...] = jnp.broadcast_to(lax.rsqrt(var + EPSILON), sums.shape)

    def norm(block):
        lanes = lanes_of(block)
        value = z_ref[:, :, :, lanes] * inv_ref[...]
        z_ref[:, :, :, lanes] = value
        zs = jnp.sum(jnp.sum(value, axis=1), axis=1)
        zsum_ref[:, lanes] = zs
        gain = full[pl.ds(BLOCK_ROW, 1), lanes]
        img = jnp.sum(isum[:, :, lanes], axis=1)
        pooled[:, lanes] = (img + zs * gain) * (1.0 / (MAP_SIDE * MAP_SIDE))

    loop(0, BLOCKS, norm)
    value = pooled[...]
    centred = value - jnp.mean(value, axis=1, keepdims=True)
    inverse = lax.rsqrt(jnp.mean(centred * centred, axis=1, keepdims=True) + EPSILON)
    poolinv_ref[...] = jnp.broadcast_to(inverse, poolinv_ref.shape)
    normed_ref[...] = centred * inverse


def loss_kernel(
    normed_ref, head_ref, proj_ref, text_ref,
    dnormed_ref, projgrad_ref, headgrad_ref, losspart_ref, gtext_ref,
    normed_s, normed_r, part_s, part_r, img_s, img_r, row_s, row_r, dimg_s, dimg_r,
    demb_s, demb_r, dn_s, dn_r, text_s, text_r, col_s, col_r, dcap_s, dcap_r,
    fs, fr, ds, dr,
):
    me_f, me_d = lax.axis_index("fsdp"), lax.axis_index("dp")

    def fex(n, source, dst):
        return Exchange("fsdp", N_FSDP, me_f, source, dst, fs.at[n], fr.at[n])

    def dex(n, source, dst):
        return Exchange("dp", N_DP, me_d, source, dst, ds.at[n], dr.at[n])

    def stack(ref, count):
        return jnp.concatenate([ref[k] for k in range(count)], axis=0)

    def total(ref, count):
        out = ref[0]
        for k in range(1, count):
            out = out + ref[k]
        return out

    def spread(ref, value):
        for k in range(ref.shape[0]):
            ref[k] = value[IMGS * k : IMGS * (k + 1)]

    text = text_ref[...].astype(F32)
    text_scale = lax.rsqrt(jnp.sum(text * text, axis=1, keepdims=True) + EPSILON)
    text_f = text * text_scale
    text_unit = text_f.astype(BF16)
    text_s[...] = text_unit
    text_r[me_d] = text_unit
    for p in range(N_FSDP // 2):
        value = normed_ref[:, 384 * p : 384 * (p + 1)]
        normed_s[2 * p] = value[:, :SHARD]
        normed_s[2 * p + 1] = value[:, SHARD:]
    normed_r[me_f] = normed_s[me_f]
    greet(me_f, me_d, True)
    x_norm = fex(0, lambda peer: normed_s.at[peer], normed_r)
    x_norm.start()
    x_text = dex(0, lambda peer: text_s, text_r)
    x_text.start()
    x_norm.wait_recv()
    normed = stack(normed_r, N_FSDP)
    head = head_ref[...]
    query = (normed * head).astype(BF16)
    part = jnp.dot(query, proj_ref[...], preferred_element_type=F32)
    spread(part_s, part)
    part_r[me_f] = part_s[me_f]
    x_part = fex(1, lambda peer: part_s.at[peer], part_r)
    x_part.start()
    x_part.wait_recv()
    embedding = total(part_r, N_FSDP)
    image_scale = lax.rsqrt(jnp.sum(embedding * embedding, axis=1, keepdims=True) + EPSILON)
    image_f = embedding * image_scale
    image_unit = image_f.astype(BF16)
    img_s[...] = image_unit
    img_r[me_f] = image_unit
    x_img = fex(2, lambda peer: img_s, img_r)
    x_img.start()
    diagonal = LOGIT_SCALE * jnp.sum(image_unit.astype(F32) * text_unit.astype(F32))
    x_text.wait_recv()
    text_cols = stack(text_r, N_DP)
    x_img.wait_recv()
    image_rows = stack(img_r, N_FSDP)
    n_row, n_col = N_FSDP * IMGS, N_DP * IMGS
    logits = LOGIT_SCALE * contract(image_rows, text_cols, 1, 1)
    exps = jnp.exp(logits)
    col_part = jnp.sum(exps, axis=0, keepdims=True)
    row_part = jnp.sum(exps, axis=1, keepdims=True)
    eye = (
        lax.broadcasted_iota(jnp.int32, (n_row, 128), 0)
        == lax.broadcasted_iota(jnp.int32, (n_row, 128), 1)
    )
    row_flat = jnp.sum(jnp.where(eye, row_part, 0.0), axis=0, keepdims=True)
    col_flat = jnp.concatenate([col_part, jnp.zeros((1, 128 - n_col), F32)], axis=1)
    col_s[...] = col_flat
    col_r[me_d] = col_flat
    x_col = dex(1, lambda peer: col_s, col_r)
    x_col.start()
    row_s[...] = row_flat
    row_r[me_f] = row_flat
    x_row = fex(3, lambda peer: row_s, row_r)
    x_row.start()
    x_row.wait_recv()
    row_sum = total(row_r, N_FSDP)
    row_lse = jnp.log(jnp.sum(jnp.where(eye, row_sum, 0.0), axis=1, keepdims=True))
    row_term = jnp.exp(logits - row_lse)
    at_row = lax.broadcasted_iota(jnp.int32, (n_row, n_col), 0)
    at_col = lax.broadcasted_iota(jnp.int32, (n_row, n_col), 1)
    pair = jnp.where(
        (at_row - IMGS * me_f == at_col - IMGS * me_d)
        & (at_row >= IMGS * me_f)
        & (at_row < IMGS * me_f + IMGS),
        2.0,
        0.0,
    )
    x_col.wait_recv()
    col_lse = jnp.log(total(col_r, N_DP)[:, :n_col])
    weights = (row_term + jnp.exp(logits - col_lse) - pair).astype(BF16)
    dimg = jnp.dot(weights, text_cols, preferred_element_type=F32)
    spread(dimg_s, dimg)
    dimg_r[me_f] = dimg_s[me_f]
    x_dimg = fex(4, lambda peer: dimg_s.at[peer], dimg_r)
    x_dimg.start()
    dcap = contract(weights, image_rows, 0, 0)
    spread(dcap_s, dcap)
    dcap_r[me_d] = dcap_s[me_d]
    x_dcap = dex(2, lambda peer: dcap_s.at[peer], dcap_r)
    x_dcap.start()
    loss_part = (
        jnp.sum(row_lse) * (1.0 / N_FSDP) + jnp.sum(col_lse) * (1.0 / N_DP) - 2.0 * diagonal
    )
    losspart_ref[...] = jnp.full(losspart_ref.shape, loss_part, F32)
    x_dimg.wait_recv()
    d_image = 7.0 * total(dimg_r, N_FSDP)
    d_embedding = (
        image_scale * (d_image - image_f * jnp.sum(image_f * d_image, axis=1, keepdims=True))
    ).astype(BF16)
    demb_s[...] = d_embedding
    demb_r[me_f] = d_embedding
    x_demb = fex(5, lambda peer: demb_s, demb_r)
    x_demb.start()
    x_demb.wait_recv()
    demb = stack(demb_r, N_FSDP)
    d_query = contract(demb, proj_ref[...], 1, 1)
    spread(dn_s, d_query * head)
    dn_r[me_f] = dn_s[me_f]
    x_dn = fex(6, lambda peer: dn_s.at[peer], dn_r)
    x_dn.start()
    headgrad_ref[...] = jnp.sum(d_query * normed, axis=0, keepdims=True)
    projgrad_ref[...] = contract(query, demb, 0, 0)
    x_dcap.wait_recv()
    d_caption = 7.0 * total(dcap_r, N_DP)
    gtext_ref[...] = text_scale * (
        d_caption - text_f * jnp.sum(text_f * d_caption, axis=1, keepdims=True)
    )
    x_dn.wait_recv()

    def write(p, value):
        dnormed_ref[:, 384 * p : 384 * (p + 1)] = value

    join_pairs(lambda k: dn_r[k], write)
    for ex in (x_norm, x_text, x_part, x_img, x_col, x_row, x_dimg, x_dcap, x_demb, x_dn):
        ex.wait_send()


def backward_kernel(
    images, z_ref, inv_ref, full, zsum_ref, dnormed_ref, normed_ref, poolinv_ref, losspart_ref,
    gimg_ref, blocks_ref,
    grads, dh, dn, sums, mean1,
):
    margin = KERNEL // 2
    normed = normed_ref[...]
    d_normed = dnormed_ref[...]
    d_pooled = poolinv_ref[:, :1] * (
        d_normed
        - jnp.mean(d_normed, axis=1, keepdims=True)
        - normed * jnp.mean(d_normed * normed, axis=1, keepdims=True)
    )
    d_hidden = d_pooled * (1.0 / (MAP_SIDE * MAP_SIDE))
    dh[...] = d_hidden
    d_norm = d_hidden * full[BLOCK_ROW : BLOCK_ROW + 1, :]
    dn[...] = d_norm
    grads[ROWS - 8 :, :] = jnp.zeros((8, CHANNELS), F32)
    grads[BLOCK_ROW : BLOCK_ROW + 1, :] = jnp.sum(d_hidden * zsum_ref[...], axis=0, keepdims=True)
    grads[LOSS_ROW : LOSS_ROW + 1, :] = jnp.broadcast_to(losspart_ref[:, :1], (1, CHANNELS))
    mean1[...] = jnp.broadcast_to(jnp.mean(d_norm, axis=1, keepdims=True), mean1.shape)
    sums[...] = jnp.zeros_like(sums)

    def project(block):
        lanes = lanes_of(block)
        for b in range(IMGS):
            row = jnp.broadcast_to(dn[pl.ds(b, 1), lanes], (MAP_SIDE, 128))
            for i in range(MAP_SIDE):
                sums[b, i] += row * z_ref[b, i, :, lanes]

    loop(0, BLOCKS, project)
    mean2 = jnp.sum(sums[...], axis=3, keepdims=True) * (1.0 / CHANNELS)
    sums[...] = jnp.broadcast_to(mean2, sums.shape)

    def conv(block):
        lanes = lanes_of(block)
        maps, pixels, acc = [], [], []
        bias = None
        for b in range(IMGS):
            row = jnp.broadcast_to(dn[pl.ds(b, 1), lanes], (MAP_SIDE, 128)) - jnp.broadcast_to(
                mean1[pl.ds(b, 1), :], (MAP_SIDE, 128)
            )
            hidden = jnp.broadcast_to(dh[pl.ds(b, 1), lanes], (MAP_SIDE, 128))
            for i in range(MAP_SIDE):
                value = inv_ref[b, i] * (row - z_ref[b, i, :, lanes] * sums[b, i])
                maps.append(value)
                bias = value if bias is None else bias + value
                pixels.append(images[b, i, :, lanes].astype(F32))
                acc.append(hidden)
        grads[pl.ds(BIAS_ROW, 1), lanes] = jnp.sum(bias, axis=0, keepdims=True)
        for s in range(KERNEL):
            cols = [shifted(value, s - margin) for value in maps]
            for r in range(KERNEL):
                tap = jnp.broadcast_to(full[pl.ds(r * KERNEL + s, 1), lanes], (MAP_SIDE, 128))
                grad = None
                for b in range(IMGS):
                    for i in range(MAP_SIDE):
                        if 0 <= i - r + margin < MAP_SIDE:
                            col = cols[b * MAP_SIDE + i - r + margin]
                            k = b * MAP_SIDE + i
                            acc[k] = acc[k] + col * tap
                            term = col * pixels[k]
                            grad = term if grad is None else grad + term
                grads[pl.ds(r * KERNEL + s, 1), lanes] = jnp.sum(grad, axis=0, keepdims=True)
        for b in range(IMGS):
            for i in range(MAP_SIDE):
                gimg_ref[b, i, :, lanes] = acc[b * MAP_SIDE + i].astype(BF16)

    loop(0, BLOCKS, conv)
    for p in range(N_FSDP // 2):
        value = grads[:, 384 * p : 384 * (p + 1)]
        blocks_ref[2 * p] = value[:, :SHARD]
        blocks_ref[2 * p + 1] = value[:, SHARD:]


PROJ_OWNERS = SHARD // 8
SMALL_OWNERS = ROWS // 8


def reduce_kernel(
    blocks_ref, headgrad_ref, projgrad_ref, small_ref, proj_ref,
    held_r, small, proj_r, small_r, proj_mine, small_mine, proj_all, small_all,
    fs, fr, ps, pr, ss, sr, gs, gr,
):
    me_f, me_d = lax.axis_index("fsdp"), lax.axis_index("dp")
    held_r[me_f] = blocks_ref[me_f]
    greet(me_f, me_d, True)
    first = PROJ_OWNERS
    last = PROJ_OWNERS + SMALL_OWNERS

    def proj_rows(k):
        return pl.ds(pl.multiple_of(k * 8, 8), 8)

    def small_rows(k):
        return pl.ds(pl.multiple_of((k - first) * 8, 8), 8)

    def peers(act):
        def body(t):
            act(t, lax.rem(me_d + t, N_DP))

        loop(1, N_DP, body)

    def proj_copy(t, peer, to):
        return copy_to("dp", peer, projgrad_ref.at[proj_rows(to)], proj_r.at[me_d], ps.at[t], pr.at[me_d])

    def small_copy(t, peer, to):
        return copy_to("dp", peer, small.at[small_rows(to)], small_r.at[me_d], ss.at[t], sr.at[me_d])

    def start_proj(t, peer):
        @pl.when(peer < first)
        def _():
            proj_copy(t, peer, peer).start()

    peers(start_proj)
    ex = Exchange("fsdp", N_FSDP, me_f, lambda peer: blocks_ref.at[peer], held_r, fs, fr)
    ex.start()
    ex.wait_recv()
    held = held_r[0]
    for k in range(1, N_FSDP):
        held = held + held_r[k]
    small[...] = held
    small[HEAD_ROW : HEAD_ROW + 1, :] = headgrad_ref[...]

    def start_small(t, peer):
        @pl.when((peer >= first) & (peer < last))
        def _():
            small_copy(t, peer, peer).start()

    peers(start_small)

    def all_copy(t, peer, sender, mine, everyone, slot):
        return copy_to("dp", peer, mine, everyone.at[slot], gs.at[t], gr.at[sender])

    @pl.when(me_d < first)
    def _():
        proj_r[me_d] = projgrad_ref[proj_rows(me_d), :]

        def wait(t, peer):
            copy_to(
                "dp", peer, projgrad_ref.at[proj_rows(0)], proj_r.at[peer], ps.at[t], pr.at[peer]
            ).wait_recv()

        peers(wait)
        out = proj_r[0]
        for k in range(1, N_DP):
            out = out + proj_r[k]
        proj_mine[...] = out
        proj_all[me_d] = out
        peers(lambda t, peer: all_copy(t, peer, me_d, proj_mine, proj_all, me_d).start())

    @pl.when((me_d >= first) & (me_d < last))
    def _():
        small_r[me_d] = small[small_rows(me_d), :]

        def wait(t, peer):
            copy_to(
                "dp", peer, small.at[small_rows(first)], small_r.at[peer], ss.at[t], sr.at[peer]
            ).wait_recv()

        peers(wait)
        out = small_r[0]
        for k in range(1, N_DP):
            out = out + small_r[k]
        small_mine[...] = out
        small_all[me_d - first] = out
        peers(lambda t, peer: all_copy(t, peer, me_d, small_mine, small_all, me_d - first).start())

    def wait_all(t, peer):
        @pl.when(peer < first)
        def _():
            all_copy(t, peer, peer, proj_mine, proj_all, peer).wait_recv()

        @pl.when((peer >= first) & (peer < last))
        def _():
            all_copy(t, peer, peer, small_mine, small_all, peer - first).wait_recv()

    peers(wait_all)
    for k in range(PROJ_OWNERS):
        proj_ref[8 * k : 8 * (k + 1), :] = proj_all[k]
    for k in range(SMALL_OWNERS):
        small_ref[8 * k : 8 * (k + 1), :] = small_all[k]
    ex.wait_send()

    def drain(t, peer):
        @pl.when(peer < first)
        def _():
            proj_copy(t, peer, peer).wait_send()

        @pl.when((peer >= first) & (peer < last))
        def _():
            small_copy(t, peer, peer).wait_send()

        @pl.when(me_d < first)
        def _():
            all_copy(t, peer, me_d, proj_mine, proj_all, me_d).wait_send()

        @pl.when((me_d >= first) & (me_d < last))
        def _():
            all_copy(t, peer, me_d, small_mine, small_all, me_d - first).wait_send()

    peers(drain)


def call(kernel, inputs, outs, scratch, collective=None):
    params = dict(vmem_limit_bytes=48 * 1024 * 1024)
    if collective is not None:
        params.update(collective_id=collective, has_side_effects=True)
    return pl.pallas_call(
        kernel,
        out_shape=[jax.ShapeDtypeStruct(s, d) for s, d in outs],
        in_specs=[VMEM_SPEC] * len(inputs),
        out_specs=[VMEM_SPEC] * len(outs),
        scratch_shapes=scratch,
        compiler_params=pltpu.CompilerParams(**params),
    )(*inputs)


def dma(*shape):
    return pltpu.SemaphoreType.DMA(shape)


def local(images, dw_weight, dw_bias, block_gain, head_gain, projection, text):
    V = pltpu.VMEM
    maps = (IMGS, MAP_SIDE, MAP_SIDE, CHANNELS)
    lanes = (IMGS, MAP_SIDE, MAP_SIDE, 128)
    wide = (IMGS, CHANNELS)
    (full,) = call(
        gather_kernel,
        (dw_weight, dw_bias[None], block_gain[None]),
        [((ROWS, CHANNELS), F32)],
        [V((ROWS, SHARD), F32), V((N_FSDP, ROWS, SHARD), F32), dma(N_FSDP), dma(N_FSDP)],
        0,
    )
    z, inv, zsum, normed, poolinv = call(
        forward_kernel,
        (images, full),
        [(maps, F32), (lanes, F32), (wide, F32), (wide, F32), ((IMGS, 128), F32)],
        [V(lanes, F32), V((IMGS, MAP_SIDE, CHANNELS), F32), V(wide, F32)],
    )
    two = (IMGS, EMBED)
    f_blocks = lambda shape, kind: V((N_FSDP,) + shape, kind)
    d_blocks = lambda shape, kind: V((N_DP,) + shape, kind)
    dnormed, projgrad, headgrad, losspart, grad_text = call(
        loss_kernel,
        (normed, head_gain[None], projection, text),
        [(wide, F32), ((SHARD, EMBED), F32), ((1, SHARD), F32), ((1, 128), F32), (two, F32)],
        [
            f_blocks((IMGS, SHARD), F32), f_blocks((IMGS, SHARD), F32),
            f_blocks(two, F32), f_blocks(two, F32),
            V(two, BF16), f_blocks(two, BF16),
            V((1, 128), F32), f_blocks((1, 128), F32),
            f_blocks(two, F32), f_blocks(two, F32),
            V(two, BF16), f_blocks(two, BF16),
            f_blocks((IMGS, SHARD), F32), f_blocks((IMGS, SHARD), F32),
            V(two, BF16), d_blocks(two, BF16),
            V((1, 128), F32), d_blocks((1, 128), F32),
            d_blocks(two, F32), d_blocks(two, F32),
            dma(7, N_FSDP), dma(7, N_FSDP), dma(3, N_DP), dma(3, N_DP),
        ],
        1,
    )
    grad_images, blocks = call(
        backward_kernel,
        (images, z, inv, full, zsum, dnormed, normed, poolinv, losspart),
        [(maps, BF16), ((N_FSDP, ROWS, SHARD), F32)],
        [V((ROWS, CHANNELS), F32), V(wide, F32), V(wide, F32), V(lanes, F32), V((IMGS, 128), F32)],
    )
    sums, sum_proj = call(
        reduce_kernel,
        (blocks, headgrad, projgrad),
        [((ROWS, SHARD), F32), ((SHARD, EMBED), F32)],
        [
            f_blocks((ROWS, SHARD), F32), V((ROWS, SHARD), F32),
            d_blocks((8, EMBED), F32), d_blocks((8, SHARD), F32),
            V((8, EMBED), F32), V((8, SHARD), F32),
            V((PROJ_OWNERS, 8, EMBED), F32), V((SMALL_OWNERS, 8, SHARD), F32),
            dma(N_FSDP), dma(N_FSDP), dma(N_DP), dma(N_DP), dma(N_DP), dma(N_DP), dma(N_DP), dma(N_DP),
        ],
        2,
    )
    return (
        sums[LOSS_ROW, 0] / (2.0 * N_DP * N_FSDP * IMGS),
        grad_images,
        sums[: KERNEL * KERNEL],
        sums[BIAS_ROW],
        sums[BLOCK_ROW],
        sums[HEAD_ROW],
        sum_proj,
        grad_text,
    )


def solution(mesh):
    return jax.shard_map(
        local,
        mesh=mesh,
        in_specs=(
            P(("dp", "fsdp"), None, None, None),
            P(None, "fsdp"),
            P("fsdp"),
            P("fsdp"),
            P("fsdp"),
            P("fsdp", None),
            P(("dp", "fsdp"), None),
        ),
        out_specs=(
            P(),
            P(("dp", "fsdp"), None, None, None),
            P(None, "fsdp"),
            P("fsdp"),
            P("fsdp"),
            P("fsdp"),
            P("fsdp", None),
            P(("dp", "fsdp"), None),
        ),
        check_vma=False,
    )
```

```python
import jax
import jax.numpy as jnp
from jax import lax
from jax.experimental import pallas as pl
from jax.experimental.pallas import tpu as pltpu
from jax.sharding import PartitionSpec as P

KERNEL = 7
MAP_SIDE = 8
LOGIT_SCALE = 14.0
EPSILON = 1e-06
MESH = pl.DeviceIdType.MESH
F32 = jnp.float32
BF16 = jnp.bfloat16
N_DP = 32
N_FSDP = 16
IMGS = 2
CHANNELS = 3072
SHARD = 192
EMBED = 512
ROWS = 56
BIAS_ROW, BLOCK_ROW, HEAD_ROW, LOSS_ROW = 49, 50, 51, 52
BLOCKS = CHANNELS // 128
VMEM_SPEC = pl.BlockSpec(memory_space=pltpu.VMEM)


def contract(left, right, left_dim, right_dim):
    return lax.dot_general(
        left, right, (((left_dim,), (right_dim,)), ((), ())), preferred_element_type=F32
    )


def copy_to(axis, peer, src, dst, send_sem, recv_sem):
    return pltpu.make_async_remote_copy(
        src_ref=src,
        dst_ref=dst,
        send_sem=send_sem,
        recv_sem=recv_sem,
        device_id={axis: peer},
        device_id_type=MESH,
    )


def loop(low, high, body):
    def step(t, carry):
        body(t)
        return carry

    lax.fori_loop(low, high, step, 0)


def greet(me_f, me_d):
    barrier = pltpu.get_barrier_semaphore()

    def signal(axis, me, count):
        def body(t):
            peer = lax.rem(me + t, count)
            pl.semaphore_signal(barrier, inc=1, device_id={axis: peer}, device_id_type=MESH)

        loop(1, count, body)

    signal("dp", me_d, N_DP)
    signal("fsdp", me_f, N_FSDP)


def greeted():
    pl.semaphore_wait(pltpu.get_barrier_semaphore(), N_FSDP + N_DP - 2)


class Exchange:
    def __init__(self, axis, count, me, source, dst, send_sem, recv_sem):
        self.axis, self.count, self.me = axis, count, me
        self.source, self.dst, self.send_sem, self.recv_sem = source, dst, send_sem, recv_sem

    def _each(self, act):
        def body(t):
            act(t, lax.rem(self.me + t, self.count))

        loop(1, self.count, body)

    def start(self):
        def act(t, peer):
            copy_to(
                self.axis, peer, self.source(peer), self.dst.at[self.me],
                self.send_sem.at[t], self.recv_sem.at[self.me],
            ).start()

        self._each(act)

    def wait_recv(self):
        def act(t, peer):
            copy_to(
                self.axis, peer, self.source(peer), self.dst.at[peer],
                self.send_sem.at[t], self.recv_sem.at[peer],
            ).wait_recv()

        self._each(act)

    def wait_recv_from(self, sender):
        copy_to(
            self.axis, sender, self.source(sender), self.dst.at[sender],
            self.send_sem.at[0], self.recv_sem.at[sender],
        ).wait_recv()

    def wait_send(self):
        def act(t, peer):
            copy_to(
                self.axis, peer, self.source(peer), self.dst.at[self.me],
                self.send_sem.at[t], self.recv_sem.at[self.me],
            ).wait_send()

        self._each(act)


def join_pairs(read, write):
    for p in range(N_FSDP // 2):
        write(p, jnp.concatenate([read(2 * p), read(2 * p + 1)], axis=1))


def shifted(value, amount):
    if amount == 0:
        return value
    place = lax.broadcasted_iota(jnp.int32, value.shape, 0)
    rolled = pltpu.roll(value, amount % MAP_SIDE, 0)
    inside = place >= amount if amount > 0 else place < MAP_SIDE + amount
    return jnp.where(inside, rolled, 0.0)


def lanes_of(block):
    return pl.ds(pl.multiple_of(block * 128, 128), 128)


PAIRS = N_FSDP // 2
PROJ_OWNERS = SHARD // 8
SMALL_OWNERS = ROWS // 8


def pair_lanes(p):
    return pl.ds(pl.multiple_of(p * (2 * SHARD), 128), 2 * SHARD)


def stack(ref, count):
    return jnp.concatenate([ref[k] for k in range(count)], axis=0)


def total(ref, count):
    out = ref[0]
    for k in range(1, count):
        out = out + ref[k]
    return out


def spread(ref, value):
    for k in range(ref.shape[0]):
        ref[k] = value[IMGS * k : IMGS * (k + 1)]


def forward_block(block, images, full, z, sums, isum):
    margin = KERNEL // 2
    lanes = lanes_of(block)
    for b in range(IMGS):
        rows = [images[b, i, :, lanes].astype(F32) for i in range(MAP_SIDE)]
        pixels = rows[0]
        for i in range(1, MAP_SIDE):
            pixels = pixels + rows[i]
        isum[b, :, lanes] = pixels
        bias = jnp.broadcast_to(full[pl.ds(BIAS_ROW, 1), lanes], (MAP_SIDE, 128))
        acc = [bias] * MAP_SIDE
        for s in range(KERNEL):
            cols = [shifted(row, margin - s) for row in rows]
            for r in range(KERNEL):
                tap = jnp.broadcast_to(full[pl.ds(r * KERNEL + s, 1), lanes], (MAP_SIDE, 128))
                for i in range(MAP_SIDE):
                    if 0 <= i + r - margin < MAP_SIDE:
                        acc[i] = acc[i] + cols[i + r - margin] * tap
        for i in range(MAP_SIDE):
            z[b, i, :, lanes] = acc[i]
            sums[b, i] += acc[i]


def forward_norm(full, z, inv, zsum, sums, isum, pooled):
    mean = jnp.sum(sums[...], axis=3, keepdims=True) * (1.0 / CHANNELS)
    inv[...] = jnp.broadcast_to(mean, sums.shape)
    sums[...] = jnp.zeros_like(sums)

    def centre(block):
        lanes = lanes_of(block)
        value = z[:, :, :, lanes] - inv[...]
        z[:, :, :, lanes] = value
        sums[...] += value * value

    loop(0, BLOCKS, centre)
    var = jnp.sum(sums[...], axis=3, keepdims=True) * (1.0 / CHANNELS)
    inv[...] = jnp.broadcast_to(lax.rsqrt(var + EPSILON), sums.shape)

    def norm(block):
        lanes = lanes_of(block)
        value = z[:, :, :, lanes] * inv[...]
        z[:, :, :, lanes] = value
        zs = jnp.sum(jnp.sum(value, axis=1), axis=1)
        zsum[:, lanes] = zs
        gain = full[pl.ds(BLOCK_ROW, 1), lanes]
        img = jnp.sum(isum[:, :, lanes], axis=1)
        pooled[:, lanes] = (img + zs * gain) * (1.0 / (MAP_SIDE * MAP_SIDE))

    loop(0, BLOCKS, norm)
    value = pooled[...]
    centred = value - jnp.mean(value, axis=1, keepdims=True)
    inverse = lax.rsqrt(jnp.mean(centred * centred, axis=1, keepdims=True) + EPSILON)
    return centred * inverse, inverse


def backward_block(block, images, z, inv, full, dh, dn, sums, mean1, grads, gimg):
    margin = KERNEL // 2
    lanes = lanes_of(block)
    maps, pixels, acc = [], [], []
    bias = None
    for b in range(IMGS):
        row = jnp.broadcast_to(dn[pl.ds(b, 1), lanes], (MAP_SIDE, 128)) - jnp.broadcast_to(
            mean1[pl.ds(b, 1), :], (MAP_SIDE, 128)
        )
        hidden = jnp.broadcast_to(dh[pl.ds(b, 1), lanes], (MAP_SIDE, 128))
        for i in range(MAP_SIDE):
            value = inv[b, i] * (row - z[b, i, :, lanes] * sums[b, i])
            maps.append(value)
            bias = value if bias is None else bias + value
            pixels.append(images[b, i, :, lanes].astype(F32))
            acc.append(hidden)
    grads[pl.ds(BIAS_ROW, 1), lanes] = jnp.sum(bias, axis=0, keepdims=True)
    for s in range(KERNEL):
        cols = [shifted(value, s - margin) for value in maps]
        for r in range(KERNEL):
            tap = jnp.broadcast_to(full[pl.ds(r * KERNEL + s, 1), lanes], (MAP_SIDE, 128))
            grad = None
            for b in range(IMGS):
                for i in range(MAP_SIDE):
                    if 0 <= i - r + margin < MAP_SIDE:
                        col = cols[b * MAP_SIDE + i - r + margin]
                        k = b * MAP_SIDE + i
                        acc[k] = acc[k] + col * tap
                        term = col * pixels[k]
                        grad = term if grad is None else grad + term
            grads[pl.ds(r * KERNEL + s, 1), lanes] = jnp.sum(grad, axis=0, keepdims=True)
    for b in range(IMGS):
        for i in range(MAP_SIDE):
            gimg[b, i, :, lanes] = acc[b * MAP_SIDE + i].astype(BF16)


def step_kernel(
    images_hbm, w_hbm, bias_hbm, gain_hbm, head_hbm, proj_hbm, text_hbm,
    gimg_hbm, small_out, proj_out, gtext_out,
    images, w_in, bias_in, gain_in, head_in, proj_in, text_in,
    pack, held, full, z, inv, zsum, sums, isum, pooled,
    normed_s, normed_r, part_s, part_r, img_s, img_r, row_s, row_r, dimg_s, dimg_r,
    demb_s, demb_r, dn_s, dn_r, text_s, text_r, col_s, col_r, dcap_s, dcap_r,
    dnormed, projgrad, grads, dh, dn, mean1, gimg, blocks_s, blocks_r,
    small, proj_r, small_r, proj_mine, small_mine, proj_all, small_all,
    load_sem, fs, fr, ds, dr, ps, pr, ss, sr, gs, gr,
):
    me_f, me_d = lax.axis_index("fsdp"), lax.axis_index("dp")
    my_pair = lax.div(me_f, 2)
    greet(me_f, me_d)
    loads = [
        pltpu.make_async_copy(src, dst, load_sem.at[n])
        for n, (src, dst) in enumerate(
            (
                (w_hbm, w_in), (bias_hbm, bias_in), (gain_hbm, gain_in), (text_hbm, text_in),
                (images_hbm, images), (head_hbm, head_in), (proj_hbm, proj_in),
            )
        )
    ]
    for load in loads:
        load.start()

    def fex(n, source, dst):
        return Exchange("fsdp", N_FSDP, me_f, source, dst, fs.at[n], fr.at[n])

    def dex(n, source, dst):
        return Exchange("dp", N_DP, me_d, source, dst, ds.at[n], dr.at[n])

    sums[...] = jnp.zeros_like(sums)
    for load in loads[:4]:
        load.wait()
    rows = jnp.concatenate(
        [w_in[...], bias_in[...], gain_in[...], jnp.zeros((ROWS - 51, SHARD), F32)], axis=0
    )
    pack[...] = rows
    held[me_f] = rows
    text = text_in[...].astype(F32)
    text_scale = lax.rsqrt(jnp.sum(text * text, axis=1, keepdims=True) + EPSILON)
    text_f = text * text_scale
    text_unit = text_f.astype(BF16)
    text_s[...] = text_unit
    text_r[me_d] = text_unit
    greeted()
    x_pack = fex(7, lambda peer: pack, held)
    x_pack.start()
    x_text = dex(0, lambda peer: text_s, text_r)
    x_text.start()
    for load in loads[4:]:
        load.wait()

    def forward_pair(t):
        p = lax.rem(my_pair - t + PAIRS, PAIRS)
        for c in range(2):

            @pl.when(2 * p + c != me_f)
            def _():
                x_pack.wait_recv_from(2 * p + c)

        full[:, pair_lanes(p)] = jnp.concatenate([held[2 * p], held[2 * p + 1]], axis=1)
        loop(0, 3, lambda k: forward_block(3 * p + k, images, full, z, sums, isum))

    loop(0, PAIRS, forward_pair)
    pool_normed, pool_inverse = forward_norm(full, z, inv, zsum, sums, isum, pooled)

    for p in range(PAIRS):
        value = pool_normed[:, 384 * p : 384 * (p + 1)]
        normed_s[2 * p] = value[:, :SHARD]
        normed_s[2 * p + 1] = value[:, SHARD:]
    pooled[...] = pool_normed
    normed_r[me_f] = normed_s[me_f]
    x_norm = fex(0, lambda peer: normed_s.at[peer], normed_r)
    x_norm.start()
    x_text.wait_recv()
    text_cols = stack(text_r, N_DP)
    x_norm.wait_recv()
    normed = stack(normed_r, N_FSDP)
    head = head_in[...]
    query = (normed * head).astype(BF16)
    part = jnp.dot(query, proj_in[...], preferred_element_type=F32)
    spread(part_s, part)
    part_r[me_f] = part_s[me_f]
    x_part = fex(1, lambda peer: part_s.at[peer], part_r)
    x_part.start()
    x_part.wait_recv()
    embedding = total(part_r, N_FSDP)
    image_scale = lax.rsqrt(jnp.sum(embedding * embedding, axis=1, keepdims=True) + EPSILON)
    image_f = embedding * image_scale
    image_unit = image_f.astype(BF16)
    img_s[...] = image_unit
    img_r[me_f] = image_unit
    x_img = fex(2, lambda peer: img_s, img_r)
    x_img.start()
    diagonal = LOGIT_SCALE * jnp.sum(image_unit.astype(F32) * text_unit.astype(F32))

    n_row, n_col = N_FSDP * IMGS, N_DP * IMGS
    eye = (
        lax.broadcasted_iota(jnp.int32, (n_row, 128), 0)
        == lax.broadcasted_iota(jnp.int32, (n_row, 128), 1)
    )
    x_img.wait_recv()
    image_rows = stack(img_r, N_FSDP)
    logits = LOGIT_SCALE * contract(image_rows, text_cols, 1, 1)
    exps = jnp.exp(logits)
    col_part = jnp.sum(exps, axis=0, keepdims=True)
    col_flat = jnp.concatenate([col_part, jnp.zeros((1, 128 - n_col), F32)], axis=1)
    col_s[...] = col_flat
    col_r[me_d] = col_flat
    x_col = dex(1, lambda peer: col_s, col_r)
    x_col.start()
    row_part = jnp.sum(exps, axis=1, keepdims=True)
    row_flat = jnp.sum(jnp.where(eye, row_part, 0.0), axis=0, keepdims=True)
    row_s[...] = row_flat
    row_r[me_f] = row_flat
    x_row = fex(3, lambda peer: row_s, row_r)
    x_row.start()
    x_row.wait_recv()
    row_sum = total(row_r, N_FSDP)
    row_lse = jnp.log(jnp.sum(jnp.where(eye, row_sum, 0.0), axis=1, keepdims=True))
    row_term = jnp.exp(logits - row_lse)
    at_row = lax.broadcasted_iota(jnp.int32, (n_row, n_col), 0)
    at_col = lax.broadcasted_iota(jnp.int32, (n_row, n_col), 1)
    pair = jnp.where(
        (at_row - IMGS * me_f == at_col - IMGS * me_d)
        & (at_row >= IMGS * me_f)
        & (at_row < IMGS * me_f + IMGS),
        2.0,
        0.0,
    )
    x_col.wait_recv()
    col_lse = jnp.log(total(col_r, N_DP)[:, :n_col])
    weights = (row_term + jnp.exp(logits - col_lse) - pair).astype(BF16)
    dimg = jnp.dot(weights, text_cols, preferred_element_type=F32)
    spread(dimg_s, dimg)
    dimg_r[me_f] = dimg_s[me_f]
    x_dimg = fex(4, lambda peer: dimg_s.at[peer], dimg_r)
    x_dimg.start()
    dcap = contract(weights, image_rows, 0, 0)
    spread(dcap_s, dcap)
    dcap_r[me_d] = dcap_s[me_d]
    x_dcap = dex(2, lambda peer: dcap_s.at[peer], dcap_r)
    x_dcap.start()
    loss_part = (
        jnp.sum(row_lse) * (1.0 / N_FSDP) + jnp.sum(col_lse) * (1.0 / N_DP) - 2.0 * diagonal
    )
    x_dimg.wait_recv()
    d_image = 7.0 * total(dimg_r, N_FSDP)
    d_embedding = (
        image_scale * (d_image - image_f * jnp.sum(image_f * d_image, axis=1, keepdims=True))
    ).astype(BF16)
    demb_s[...] = d_embedding
    demb_r[me_f] = d_embedding
    x_demb = fex(5, lambda peer: demb_s, demb_r)
    x_demb.start()
    x_demb.wait_recv()
    demb = stack(demb_r, N_FSDP)
    d_query = contract(demb, proj_in[...], 1, 1)
    spread(dn_s, d_query * head)
    dn_r[me_f] = dn_s[me_f]
    x_dn = fex(6, lambda peer: dn_s.at[peer], dn_r)
    x_dn.start()
    head_grad = jnp.sum(d_query * normed, axis=0, keepdims=True)
    projgrad[...] = contract(query, demb, 0, 0)

    first = PROJ_OWNERS
    last = PROJ_OWNERS + SMALL_OWNERS

    def proj_rows(k):
        return pl.ds(pl.multiple_of(k * 8, 8), 8)

    def small_rows(k):
        return pl.ds(pl.multiple_of((k - first) * 8, 8), 8)

    def peers(act):
        def body(t):
            act(t, lax.rem(me_d + t, N_DP))

        loop(1, N_DP, body)

    def proj_copy(t, peer, to):
        return copy_to("dp", peer, projgrad.at[proj_rows(to)], proj_r.at[me_d], ps.at[t], pr.at[me_d])

    def small_copy(t, peer, to):
        return copy_to("dp", peer, small.at[small_rows(to)], small_r.at[me_d], ss.at[t], sr.at[me_d])

    def start_proj(t, peer):
        @pl.when(peer < first)
        def _():
            proj_copy(t, peer, peer).start()

    peers(start_proj)

    x_dn.wait_recv()

    def write(p, value):
        dnormed[:, 384 * p : 384 * (p + 1)] = value

    join_pairs(lambda k: dn_r[k], write)

    normed = pooled[...]
    d_normed = dnormed[...]
    d_pooled = pool_inverse * (
        d_normed
        - jnp.mean(d_normed, axis=1, keepdims=True)
        - normed * jnp.mean(d_normed * normed, axis=1, keepdims=True)
    )
    d_hidden = d_pooled * (1.0 / (MAP_SIDE * MAP_SIDE))
    dh[...] = d_hidden
    d_norm = d_hidden * full[BLOCK_ROW : BLOCK_ROW + 1, :]
    dn[...] = d_norm
    grads[ROWS - 8 :, :] = jnp.zeros((8, CHANNELS), F32)
    grads[BLOCK_ROW : BLOCK_ROW + 1, :] = jnp.sum(d_hidden * zsum[...], axis=0, keepdims=True)
    grads[LOSS_ROW : LOSS_ROW + 1, :] = jnp.full((1, CHANNELS), loss_part, F32)
    mean1[...] = jnp.broadcast_to(jnp.mean(d_norm, axis=1, keepdims=True), mean1.shape)
    sums[...] = jnp.zeros_like(sums)

    def project(block):
        lanes = lanes_of(block)
        for b in range(IMGS):
            row = jnp.broadcast_to(dn[pl.ds(b, 1), lanes], (MAP_SIDE, 128))
            for i in range(MAP_SIDE):
                sums[b, i] += row * z[b, i, :, lanes]

    loop(0, BLOCKS, project)
    mean2 = jnp.sum(sums[...], axis=3, keepdims=True) * (1.0 / CHANNELS)
    sums[...] = jnp.broadcast_to(mean2, sums.shape)

    def block_copy(owner):
        return copy_to(
            "fsdp", owner, blocks_s.at[owner], blocks_r.at[me_f], fs.at[8, owner], fr.at[8, me_f]
        )

    def backward_pair(t):
        p = lax.rem(my_pair + t, PAIRS)
        loop(
            0, 3,
            lambda k: backward_block(
                3 * p + k, images, z, inv, full, dh, dn, sums, mean1, grads, gimg
            ),
        )
        value = grads[:, pair_lanes(p)]
        for c in range(2):
            owner = 2 * p + c
            blocks_s[owner] = value[:, SHARD * c : SHARD * (c + 1)]

            @pl.when(owner != me_f)
            def _():
                block_copy(owner).start()

    loop(1, PAIRS + 1, backward_pair)
    store = pltpu.make_async_copy(gimg, gimg_hbm, load_sem.at[7])
    store.start()
    blocks_r[me_f] = blocks_s[me_f]

    def senders(act):
        loop(1, N_FSDP, lambda t: act(lax.rem(me_f - t + N_FSDP, N_FSDP)))

    senders(
        lambda s: copy_to(
            "fsdp", s, blocks_s.at[s], blocks_r.at[s], fs.at[8, s], fr.at[8, s]
        ).wait_recv()
    )
    small[...] = total(blocks_r, N_FSDP)
    small[HEAD_ROW : HEAD_ROW + 1, :] = head_grad

    def start_small(t, peer):
        @pl.when((peer >= first) & (peer < last))
        def _():
            small_copy(t, peer, peer).start()

    peers(start_small)

    def all_copy(t, peer, sender, mine, everyone, slot):
        return copy_to("dp", peer, mine, everyone.at[slot], gs.at[t], gr.at[sender])

    @pl.when(me_d < first)
    def _():
        proj_r[me_d] = projgrad[proj_rows(me_d), :]

        def wait(t, peer):
            copy_to(
                "dp", peer, projgrad.at[proj_rows(0)], proj_r.at[peer], ps.at[t], pr.at[peer]
            ).wait_recv()

        peers(wait)
        out = total(proj_r, N_DP).astype(BF16)
        proj_mine[...] = out
        proj_all[me_d] = out
        peers(lambda t, peer: all_copy(t, peer, me_d, proj_mine, proj_all, me_d).start())

    @pl.when((me_d >= first) & (me_d < last))
    def _():
        small_r[me_d] = small[small_rows(me_d), :]

        def wait(t, peer):
            copy_to(
                "dp", peer, small.at[small_rows(first)], small_r.at[peer], ss.at[t], sr.at[peer]
            ).wait_recv()

        peers(wait)
        out = total(small_r, N_DP)
        small_mine[...] = out
        small_all[me_d - first] = out
        peers(lambda t, peer: all_copy(t, peer, me_d, small_mine, small_all, me_d - first).start())

    x_dcap.wait_recv()
    d_caption = 7.0 * total(dcap_r, N_DP)
    gtext_out[...] = text_scale * (
        d_caption - text_f * jnp.sum(text_f * d_caption, axis=1, keepdims=True)
    )

    def wait_all(t, peer):
        @pl.when(peer < first)
        def _():
            all_copy(t, peer, peer, proj_mine, proj_all, peer).wait_recv()

        @pl.when((peer >= first) & (peer < last))
        def _():
            all_copy(t, peer, peer, small_mine, small_all, peer - first).wait_recv()

    peers(wait_all)
    for k in range(PROJ_OWNERS):
        proj_out[8 * k : 8 * (k + 1), :] = proj_all[k].astype(F32)
    for k in range(SMALL_OWNERS):
        small_out[8 * k : 8 * (k + 1), :] = small_all[k]

    store.wait()
    for ex in (x_pack, x_text, x_norm, x_part, x_img, x_col, x_row, x_dimg, x_dcap, x_demb, x_dn):
        ex.wait_send()

    def drain_block(owner):
        block_copy(owner).wait_send()

    senders(drain_block)

    def drain(t, peer):
        @pl.when(peer < first)
        def _():
            proj_copy(t, peer, peer).wait_send()

        @pl.when((peer >= first) & (peer < last))
        def _():
            small_copy(t, peer, peer).wait_send()

        @pl.when(me_d < first)
        def _():
            all_copy(t, peer, me_d, proj_mine, proj_all, me_d).wait_send()

        @pl.when((me_d >= first) & (me_d < last))
        def _():
            all_copy(t, peer, me_d, small_mine, small_all, me_d - first).wait_send()

    peers(drain)


def dma(*shape):
    return pltpu.SemaphoreType.DMA(shape)


def local(images, dw_weight, dw_bias, block_gain, head_gain, projection, text):
    V = pltpu.VMEM
    maps = (IMGS, MAP_SIDE, MAP_SIDE, CHANNELS)
    lanes = (IMGS, MAP_SIDE, MAP_SIDE, 128)
    wide = (IMGS, CHANNELS)
    two = (IMGS, EMBED)

    def f_blocks(shape, kind):
        return V((N_FSDP,) + shape, kind)

    def d_blocks(shape, kind):
        return V((N_DP,) + shape, kind)

    inputs = (images, dw_weight, dw_bias[None], block_gain[None], head_gain[None], projection, text)
    grad_images, sums, sum_proj, grad_text = pl.pallas_call(
        step_kernel,
        out_shape=[
            jax.ShapeDtypeStruct(shape, kind)
            for shape, kind in ((maps, BF16), ((ROWS, SHARD), F32), ((SHARD, EMBED), F32), (two, F32))
        ],
        in_specs=[pl.BlockSpec(memory_space=pl.ANY)] * len(inputs),
        out_specs=[pl.BlockSpec(memory_space=pl.ANY)] + [VMEM_SPEC] * 3,
        scratch_shapes=[
            V(maps, BF16), V((KERNEL * KERNEL, SHARD), F32), V((1, SHARD), F32), V((1, SHARD), F32),
            V((1, SHARD), F32), V((SHARD, EMBED), BF16), V(two, BF16),
            V((ROWS, SHARD), F32), f_blocks((ROWS, SHARD), F32), V((ROWS, CHANNELS), F32),
            V(maps, F32), V(lanes, F32), V(wide, F32), V(lanes, F32),
            V((IMGS, MAP_SIDE, CHANNELS), F32), V(wide, F32),
            f_blocks((IMGS, SHARD), F32), f_blocks((IMGS, SHARD), F32),
            f_blocks(two, F32), f_blocks(two, F32),
            V(two, BF16), f_blocks(two, BF16),
            V((1, 128), F32), f_blocks((1, 128), F32),
            f_blocks(two, F32), f_blocks(two, F32),
            V(two, BF16), f_blocks(two, BF16),
            f_blocks((IMGS, SHARD), F32), f_blocks((IMGS, SHARD), F32),
            V(two, BF16), d_blocks(two, BF16),
            V((1, 128), F32), d_blocks((1, 128), F32),
            d_blocks(two, F32), d_blocks(two, F32),
            V(wide, F32), V((SHARD, EMBED), F32), V((ROWS, CHANNELS), F32), V(wide, F32),
            V(wide, F32), V((IMGS, 128), F32), V(maps, BF16),
            f_blocks((ROWS, SHARD), F32), f_blocks((ROWS, SHARD), F32),
            V((ROWS, SHARD), F32), d_blocks((8, EMBED), F32), d_blocks((8, SHARD), F32),
            V((8, EMBED), BF16), V((8, SHARD), F32),
            V((PROJ_OWNERS, 8, EMBED), BF16), V((SMALL_OWNERS, 8, SHARD), F32),
            dma(8), dma(9, N_FSDP), dma(9, N_FSDP), dma(3, N_DP), dma(3, N_DP),
            dma(N_DP), dma(N_DP), dma(N_DP), dma(N_DP), dma(N_DP), dma(N_DP),
        ],
        compiler_params=pltpu.CompilerParams(
            vmem_limit_bytes=48 * 1024 * 1024, collective_id=0, has_side_effects=True
        ),
    )(*inputs)
    return (
        sums[LOSS_ROW, 0] / (2.0 * N_DP * N_FSDP * IMGS),
        grad_images,
        sums[: KERNEL * KERNEL],
        sums[BIAS_ROW],
        sums[BLOCK_ROW],
        sums[HEAD_ROW],
        sum_proj,
        grad_text,
    )


def solution(mesh):
    return jax.shard_map(
        local,
        mesh=mesh,
        in_specs=(
            P(("dp", "fsdp"), None, None, None),
            P(None, "fsdp"),
            P("fsdp"),
            P("fsdp"),
            P("fsdp"),
            P("fsdp", None),
            P(("dp", "fsdp"), None),
        ),
        out_specs=(
            P(),
            P(("dp", "fsdp"), None, None, None),
            P(None, "fsdp"),
            P("fsdp"),
            P("fsdp"),
            P("fsdp"),
            P("fsdp", None),
            P(("dp", "fsdp"), None),
        ),
        check_vma=False,
    )
```

```python
import jax
import jax.numpy as jnp
from jax import lax
from jax.experimental import pallas as pl
from jax.experimental.pallas import tpu as pltpu
from jax.sharding import PartitionSpec as P

KERNEL = 7
MAP_SIDE = 8
LOGIT_SCALE = 14.0
EPSILON = 1e-06
MESH = pl.DeviceIdType.MESH
F32 = jnp.float32
BF16 = jnp.bfloat16
N_DP = 32
N_FSDP = 16
IMGS = 2
CHANNELS = 3072
SHARD = 192
EMBED = 512
ROWS = 56
BIAS_ROW, BLOCK_ROW, HEAD_ROW, LOSS_ROW = 49, 50, 51, 52
BLOCKS = CHANNELS // 128
VMEM_SPEC = pl.BlockSpec(memory_space=pltpu.VMEM)


def contract(left, right, left_dim, right_dim):
    return lax.dot_general(
        left, right, (((left_dim,), (right_dim,)), ((), ())), preferred_element_type=F32
    )


def copy_to(axis, peer, src, dst, send_sem, recv_sem):
    return pltpu.make_async_remote_copy(
        src_ref=src,
        dst_ref=dst,
        send_sem=send_sem,
        recv_sem=recv_sem,
        device_id={axis: peer},
        device_id_type=MESH,
    )


def loop(low, high, body):
    def step(t, carry):
        body(t)
        return carry

    lax.fori_loop(low, high, step, 0)


def greet(me_f, me_d):
    barrier = pltpu.get_barrier_semaphore()

    def signal(axis, me, count):
        def body(t):
            peer = lax.rem(me + t, count)
            pl.semaphore_signal(barrier, inc=1, device_id={axis: peer}, device_id_type=MESH)

        loop(1, count, body)

    signal("dp", me_d, N_DP)
    signal("fsdp", me_f, N_FSDP)


def greeted():
    pl.semaphore_wait(pltpu.get_barrier_semaphore(), N_FSDP + N_DP - 2)


class Exchange:
    def __init__(self, axis, count, me, source, dst, send_sem, recv_sem):
        self.axis, self.count, self.me = axis, count, me
        self.source, self.dst, self.send_sem, self.recv_sem = source, dst, send_sem, recv_sem

    def start(self):
        def body(t):
            offset = 1 + lax.rem(t + self.count // 2 - 2, self.count - 1)
            peer = lax.rem(self.me + offset, self.count)
            copy_to(
                self.axis, peer, self.source(peer), self.dst.at[self.me], self.send_sem, self.recv_sem
            ).start()

        loop(0, self.count - 1, body)

    def wait_recv(self):
        wait_blocks(self.axis, self.count, self.me, self.dst, self.count - 1, None, self.recv_sem)

    def wait_send(self):
        wait_blocks(self.axis, self.count, self.me, self.dst, self.count - 1, self.send_sem, None)


def wait_blocks(axis, count, me, like, blocks, send_sem, recv_sem):
    window = like.at[pl.ds(0, blocks)]
    sem = recv_sem if send_sem is None else send_sem
    copy = copy_to(axis, lax.rem(me + 1, count), window, window, sem, sem)
    if send_sem is None:
        copy.wait_recv()
    else:
        copy.wait_send()


def join_pairs(read, write):
    for p in range(N_FSDP // 2):
        write(p, jnp.concatenate([read(2 * p), read(2 * p + 1)], axis=1))


def shifted(value, amount):
    if amount == 0:
        return value
    place = lax.broadcasted_iota(jnp.int32, value.shape, 0)
    rolled = pltpu.roll(value, amount % MAP_SIDE, 0)
    inside = place >= amount if amount > 0 else place < MAP_SIDE + amount
    return jnp.where(inside, rolled, 0.0)


def lanes_of(block):
    return pl.ds(pl.multiple_of(block * 128, 128), 128)


PAIRS = N_FSDP // 2
PROJ_OWNERS = SHARD // 8
SMALL_OWNERS = ROWS // 8


def pair_lanes(p):
    return pl.ds(pl.multiple_of(p * (2 * SHARD), 128), 2 * SHARD)


def stack(ref, count):
    return jnp.concatenate([ref[k] for k in range(count)], axis=0)


def total(ref, count):
    out = ref[0]
    for k in range(1, count):
        out = out + ref[k]
    return out


def spread(ref, value):
    for k in range(ref.shape[0]):
        ref[k] = value[IMGS * k : IMGS * (k + 1)]


def forward_block(block, images, full, z, sums, isum):
    margin = KERNEL // 2
    lanes = lanes_of(block)
    for b in range(IMGS):
        rows = [images[b, i, :, lanes].astype(F32) for i in range(MAP_SIDE)]
        pixels = rows[0]
        for i in range(1, MAP_SIDE):
            pixels = pixels + rows[i]
        isum[b, :, lanes] = pixels
        bias = jnp.broadcast_to(full[pl.ds(BIAS_ROW, 1), lanes], (MAP_SIDE, 128))
        acc = [bias] * MAP_SIDE
        for s in range(KERNEL):
            cols = [shifted(row, margin - s) for row in rows]
            for r in range(KERNEL):
                tap = jnp.broadcast_to(full[pl.ds(r * KERNEL + s, 1), lanes], (MAP_SIDE, 128))
                for i in range(MAP_SIDE):
                    if 0 <= i + r - margin < MAP_SIDE:
                        acc[i] = acc[i] + cols[i + r - margin] * tap
        for i in range(MAP_SIDE):
            z[b, i, :, lanes] = acc[i]
            sums[b, i] += acc[i]


def forward_norm(full, z, inv, zsum, sums, isum, pooled):
    mean = jnp.sum(sums[...], axis=3, keepdims=True) * (1.0 / CHANNELS)
    inv[...] = jnp.broadcast_to(mean, sums.shape)
    sums[...] = jnp.zeros_like(sums)

    def centre(block):
        lanes = lanes_of(block)
        value = z[:, :, :, lanes] - inv[...]
        z[:, :, :, lanes] = value
        sums[...] += value * value

    loop(0, BLOCKS, centre)
    var = jnp.sum(sums[...], axis=3, keepdims=True) * (1.0 / CHANNELS)
    inv[...] = jnp.broadcast_to(lax.rsqrt(var + EPSILON), sums.shape)

    def norm(block):
        lanes = lanes_of(block)
        value = z[:, :, :, lanes] * inv[...]
        z[:, :, :, lanes] = value
        zs = jnp.sum(jnp.sum(value, axis=1), axis=1)
        zsum[:, lanes] = zs
        gain = full[pl.ds(BLOCK_ROW, 1), lanes]
        img = jnp.sum(isum[:, :, lanes], axis=1)
        pooled[:, lanes] = (img + zs * gain) * (1.0 / (MAP_SIDE * MAP_SIDE))

    loop(0, BLOCKS, norm)
    value = pooled[...]
    centred = value - jnp.mean(value, axis=1, keepdims=True)
    inverse = lax.rsqrt(jnp.mean(centred * centred, axis=1, keepdims=True) + EPSILON)
    return centred * inverse, inverse


def backward_block(block, images, z, inv, full, dh, dn, sums, mean1, grads, gimg):
    margin = KERNEL // 2
    lanes = lanes_of(block)
    maps, pixels, acc = [], [], []
    bias = None
    for b in range(IMGS):
        row = jnp.broadcast_to(dn[pl.ds(b, 1), lanes], (MAP_SIDE, 128)) - jnp.broadcast_to(
            mean1[pl.ds(b, 1), :], (MAP_SIDE, 128)
        )
        hidden = jnp.broadcast_to(dh[pl.ds(b, 1), lanes], (MAP_SIDE, 128))
        for i in range(MAP_SIDE):
            value = inv[b, i] * (row - z[b, i, :, lanes] * sums[b, i])
            maps.append(value)
            bias = value if bias is None else bias + value
            pixels.append(images[b, i, :, lanes].astype(F32))
            acc.append(hidden)
    grads[pl.ds(BIAS_ROW, 1), lanes] = jnp.sum(bias, axis=0, keepdims=True)
    for s in range(KERNEL):
        cols = [shifted(value, s - margin) for value in maps]
        for r in range(KERNEL):
            tap = jnp.broadcast_to(full[pl.ds(r * KERNEL + s, 1), lanes], (MAP_SIDE, 128))
            grad = None
            for b in range(IMGS):
                for i in range(MAP_SIDE):
                    if 0 <= i - r + margin < MAP_SIDE:
                        col = cols[b * MAP_SIDE + i - r + margin]
                        k = b * MAP_SIDE + i
                        acc[k] = acc[k] + col * tap
                        term = col * pixels[k]
                        grad = term if grad is None else grad + term
            grads[pl.ds(r * KERNEL + s, 1), lanes] = jnp.sum(grad, axis=0, keepdims=True)
    for b in range(IMGS):
        for i in range(MAP_SIDE):
            gimg[b, i, :, lanes] = acc[b * MAP_SIDE + i].astype(BF16)


def step_kernel(
    images_hbm, w_hbm, bias_hbm, gain_hbm, head_hbm, proj_hbm, text_hbm,
    gimg, taps_out, bias_out, block_out, head_out, loss_out, proj_out, gtext_out,
    images, w_in, bias_in, gain_in, head_in, proj_in, text_in,
    pack, held, full, z, inv, zsum, sums, isum, pooled,
    normed_s, normed_r, part_s, part_r, img_s, img_r, row_s, row_r, dimg_s, dimg_r,
    demb_s, demb_r, dn_s, dn_r, text_s, text_r, col_s, col_r, dcap_s, dcap_r,
    dnormed, projgrad, grads, dh, dn, mean1, blocks_s, mate_r, chip_s, chip_r,
    small, proj_r, small_r, proj_mine, small_mine, proj_all, small_all,
    load_sem, fs, fr, ds, dr, ps, pr, ss, sr, gs, gr, hs, hr, near_s, near_r, far_s, far_r,
):
    me_f, me_d = lax.axis_index("fsdp"), lax.axis_index("dp")
    my_pair, core = lax.div(me_f, 2), lax.rem(me_f, 2)
    mate = 2 * my_pair + 1 - core
    greet(me_f, me_d)
    loads = [
        pltpu.make_async_copy(src, dst, load_sem.at[n])
        for n, (src, dst) in enumerate(
            (
                (w_hbm, w_in), (bias_hbm, bias_in), (gain_hbm, gain_in), (text_hbm, text_in),
                (images_hbm, images), (head_hbm, head_in), (proj_hbm, proj_in),
            )
        )
    ]
    for load in loads:
        load.start()

    def fex(n, source, dst):
        return Exchange("fsdp", N_FSDP, me_f, source, dst, fs.at[n], fr.at[n])

    def dex(n, source, dst):
        return Exchange("dp", N_DP, me_d, source, dst, ds.at[n], dr.at[n])

    sums[...] = jnp.zeros_like(sums)
    for load in loads[:4]:
        load.wait()
    rows = jnp.concatenate(
        [w_in[...], bias_in[...], gain_in[...], jnp.zeros((ROWS - 51, SHARD), F32)], axis=0
    )
    pack[...] = rows
    held[me_f] = rows
    text = text_in[...].astype(F32)
    text_scale = lax.rsqrt(jnp.sum(text * text, axis=1, keepdims=True) + EPSILON)
    text_f = text * text_scale
    text_unit = text_f.astype(BF16)
    text_s[...] = text_unit
    text_r[me_d] = text_unit
    greeted()

    def near_copy(p, block, dst):
        return copy_to("fsdp", mate, block, dst, near_s, near_r.at[p])

    def far_copy(t, n, block, dst):
        q = lax.rem(my_pair + t, PAIRS)
        return copy_to("fsdp", 2 * q + core, block, dst, far_s.at[n], far_r.at[n, my_pair])

    near_copy(my_pair, pack, held.at[me_f]).start()
    loop(1, PAIRS, lambda t: far_copy(t, 0, pack, held.at[me_f]).start())
    x_text = dex(0, lambda peer: text_s, text_r)
    x_text.start()
    for load in loads[4:]:
        load.wait()

    def hand_on(t):
        p = lax.rem(my_pair - t + PAIRS, PAIRS)
        block = held.at[2 * p + core]
        copy_to("fsdp", 2 * p + core, block, block, far_s.at[0], far_r.at[0, p]).wait_recv()
        near_copy(p, block, block).start()

    def forward_pair(t):
        p = lax.rem(my_pair - t + PAIRS, PAIRS)
        block = held.at[2 * p + 1 - core]
        near_copy(p, block, block).wait_recv()
        full[:, pair_lanes(p)] = jnp.concatenate([held[2 * p], held[2 * p + 1]], axis=1)
        loop(0, 3, lambda k: forward_block(3 * p + k, images, full, z, sums, isum))

        @pl.when(t == 0)
        def _():
            hand_on(1)

        @pl.when(t + 2 < PAIRS)
        def _():
            hand_on(t + 2)

    loop(0, PAIRS, forward_pair)
    pool_normed, pool_inverse = forward_norm(full, z, inv, zsum, sums, isum, pooled)

    for p in range(PAIRS):
        value = pool_normed[:, 384 * p : 384 * (p + 1)]
        normed_s[2 * p] = value[:, :SHARD]
        normed_s[2 * p + 1] = value[:, SHARD:]
    pooled[...] = pool_normed
    normed_r[me_f] = normed_s[me_f]
    x_norm = fex(0, lambda peer: normed_s.at[peer], normed_r)
    x_norm.start()
    x_text.wait_recv()
    text_cols = stack(text_r, N_DP)
    x_norm.wait_recv()
    normed = stack(normed_r, N_FSDP)
    head = head_in[...]
    query = (normed * head).astype(BF16)
    part = jnp.dot(query, proj_in[...], preferred_element_type=F32)
    spread(part_s, part)
    part_r[me_f] = part_s[me_f]
    x_part = fex(1, lambda peer: part_s.at[peer], part_r)
    x_part.start()
    x_part.wait_recv()
    embedding = total(part_r, N_FSDP)
    image_scale = lax.rsqrt(jnp.sum(embedding * embedding, axis=1, keepdims=True) + EPSILON)
    image_f = embedding * image_scale
    image_unit = image_f.astype(BF16)
    img_s[...] = image_unit
    img_r[me_f] = image_unit
    x_img = fex(2, lambda peer: img_s, img_r)
    x_img.start()
    diagonal = LOGIT_SCALE * jnp.sum(image_unit.astype(F32) * text_unit.astype(F32))

    n_row, n_col = N_FSDP * IMGS, N_DP * IMGS
    eye = (
        lax.broadcasted_iota(jnp.int32, (n_row, 128), 0)
        == lax.broadcasted_iota(jnp.int32, (n_row, 128), 1)
    )
    x_img.wait_recv()
    image_rows = stack(img_r, N_FSDP)
    logits = LOGIT_SCALE * contract(image_rows, text_cols, 1, 1)
    exps = jnp.exp(logits)
    col_part = jnp.sum(exps, axis=0, keepdims=True)
    col_flat = jnp.concatenate([col_part, jnp.zeros((1, 128 - n_col), F32)], axis=1)
    col_s[...] = col_flat
    col_r[me_d] = col_flat
    x_col = dex(1, lambda peer: col_s, col_r)
    x_col.start()
    row_part = jnp.sum(exps, axis=1, keepdims=True)
    row_flat = jnp.sum(jnp.where(eye, row_part, 0.0), axis=0, keepdims=True)
    row_s[...] = row_flat
    row_r[me_f] = row_flat
    x_row = fex(3, lambda peer: row_s, row_r)
    x_row.start()
    x_row.wait_recv()
    row_sum = total(row_r, N_FSDP)
    row_lse = jnp.log(jnp.sum(jnp.where(eye, row_sum, 0.0), axis=1, keepdims=True))
    row_term = jnp.exp(logits - row_lse)
    at_row = lax.broadcasted_iota(jnp.int32, (n_row, n_col), 0)
    at_col = lax.broadcasted_iota(jnp.int32, (n_row, n_col), 1)
    pair = jnp.where(
        (at_row - IMGS * me_f == at_col - IMGS * me_d)
        & (at_row >= IMGS * me_f)
        & (at_row < IMGS * me_f + IMGS),
        2.0,
        0.0,
    )
    x_col.wait_recv()
    col_lse = jnp.log(total(col_r, N_DP)[:, :n_col])
    weights = (row_term + jnp.exp(logits - col_lse) - pair).astype(BF16)
    dimg = jnp.dot(weights, text_cols, preferred_element_type=F32)
    spread(dimg_s, dimg)
    dimg_r[me_f] = dimg_s[me_f]
    x_dimg = fex(4, lambda peer: dimg_s.at[peer], dimg_r)
    x_dimg.start()
    dcap = contract(weights, image_rows, 0, 0)
    spread(dcap_s, dcap)
    dcap_r[me_d] = dcap_s[me_d]
    x_dcap = dex(2, lambda peer: dcap_s.at[peer], dcap_r)
    x_dcap.start()
    loss_part = (
        jnp.sum(row_lse) * (1.0 / N_FSDP) + jnp.sum(col_lse) * (1.0 / N_DP) - 2.0 * diagonal
    )
    x_dimg.wait_recv()
    d_image = 7.0 * total(dimg_r, N_FSDP)
    d_embedding = (
        image_scale * (d_image - image_f * jnp.sum(image_f * d_image, axis=1, keepdims=True))
    ).astype(BF16)
    demb_s[...] = d_embedding
    demb_r[me_f] = d_embedding
    x_demb = fex(5, lambda peer: demb_s, demb_r)
    x_demb.start()
    x_demb.wait_recv()
    demb = stack(demb_r, N_FSDP)
    d_query = contract(demb, proj_in[...], 1, 1)
    spread(dn_s, d_query * head)
    dn_r[me_f] = dn_s[me_f]
    x_dn = fex(6, lambda peer: dn_s.at[peer], dn_r)
    x_dn.start()
    head_grad = jnp.sum(d_query * normed, axis=0, keepdims=True)
    projgrad[...] = contract(query, demb, 0, 0)

    first = PROJ_OWNERS
    last = PROJ_OWNERS + SMALL_OWNERS

    def proj_rows(k):
        return pl.ds(pl.multiple_of(k * 8, 8), 8)

    def small_rows(k):
        return pl.ds(pl.multiple_of((k - first) * 8, 8), 8)

    def peers(act):
        def body(t):
            act(t, lax.rem(me_d + 1 + lax.rem(t + 11, N_DP - 1), N_DP))

        loop(0, N_DP - 1, body)

    def proj_copy(t, peer, to):
        return copy_to("dp", peer, projgrad.at[proj_rows(to)], proj_r.at[me_d], ps, pr)

    def small_copy(t, peer, to):
        return copy_to("dp", peer, small.at[small_rows(to)], small_r.at[me_d], ss, sr)

    def start_proj(t, peer):
        @pl.when(peer < first)
        def _():
            proj_copy(t, peer, peer).start()

    peers(start_proj)

    x_dn.wait_recv()

    def write(p, value):
        dnormed[:, 384 * p : 384 * (p + 1)] = value

    join_pairs(lambda k: dn_r[k], write)

    normed = pooled[...]
    d_normed = dnormed[...]
    d_pooled = pool_inverse * (
        d_normed
        - jnp.mean(d_normed, axis=1, keepdims=True)
        - normed * jnp.mean(d_normed * normed, axis=1, keepdims=True)
    )
    d_hidden = d_pooled * (1.0 / (MAP_SIDE * MAP_SIDE))
    dh[...] = d_hidden
    d_norm = d_hidden * full[BLOCK_ROW : BLOCK_ROW + 1, :]
    dn[...] = d_norm
    grads[ROWS - 8 :, :] = jnp.zeros((8, CHANNELS), F32)
    grads[BLOCK_ROW : BLOCK_ROW + 1, :] = jnp.sum(d_hidden * zsum[...], axis=0, keepdims=True)
    grads[LOSS_ROW : LOSS_ROW + 1, :] = jnp.full(
        (1, CHANNELS), loss_part * (0.5 / (N_DP * N_FSDP * IMGS)), F32
    )
    mean1[...] = jnp.broadcast_to(jnp.mean(d_norm, axis=1, keepdims=True), mean1.shape)
    sums[...] = jnp.zeros_like(sums)

    def project(block):
        lanes = lanes_of(block)
        for b in range(IMGS):
            row = jnp.broadcast_to(dn[pl.ds(b, 1), lanes], (MAP_SIDE, 128))
            for i in range(MAP_SIDE):
                sums[b, i] += row * z[b, i, :, lanes]

    loop(0, BLOCKS, project)
    mean2 = jnp.sum(sums[...], axis=3, keepdims=True) * (1.0 / CHANNELS)
    sums[...] = jnp.broadcast_to(mean2, sums.shape)

    def mate_copy(p):
        return copy_to(
            "fsdp", mate, blocks_s.at[2 * p + 1 - core], mate_r.at[p], hs, hr.at[p]
        )

    def chip_sum(p):
        copy_to("fsdp", mate, mate_r.at[p], mate_r.at[p], hs, hr.at[p]).wait_recv()
        return blocks_s[2 * p + core] + mate_r[p]

    def send_chip(t):
        p = lax.rem(my_pair + t, PAIRS)
        chip_s[p] = chip_sum(p)
        far_copy(t, 1, chip_s.at[p], chip_r.at[my_pair]).start()

    def backward_pair(t):
        p = lax.rem(my_pair + t, PAIRS)

        def piece(k):
            backward_block(3 * p + k, images, z, inv, full, dh, dn, sums, mean1, grads, gimg)

            @pl.when((k == 0) & (t > 1))
            def _():
                send_chip(t - 1)

        loop(0, 3, piece)
        value = grads[:, pair_lanes(p)]
        blocks_s[2 * p] = value[:, :SHARD]
        blocks_s[2 * p + 1] = value[:, SHARD:]
        mate_copy(p).start()

    loop(1, PAIRS + 1, backward_pair)
    chip_r[my_pair] = chip_sum(my_pair)

    def chip_wait(t):
        p = lax.rem(my_pair + t, PAIRS)
        copy_to(
            "fsdp", 2 * p + core, chip_r.at[p], chip_r.at[p], far_s.at[1], far_r.at[1, p]
        ).wait_recv()

    loop(1, PAIRS, chip_wait)
    small[...] = total(chip_r, PAIRS)
    small[HEAD_ROW : HEAD_ROW + 1, :] = head_grad

    def start_small(t, peer):
        @pl.when((peer >= first) & (peer < last))
        def _():
            small_copy(t, peer, peer).start()

    peers(start_small)

    def proj_all_copy(peer):
        return copy_to("dp", peer, proj_mine, proj_all.at[me_d], gs.at[0], gr.at[0])

    def small_all_copy(peer):
        return copy_to("dp", peer, small_mine, small_all.at[me_d - first], gs.at[1], gr.at[1])

    def dp_wait(like, blocks, send_sem, recv_sem):
        wait_blocks("dp", N_DP, me_d, like, blocks, send_sem, recv_sem)

    owns_proj = me_d < first
    owns_small = (me_d >= first) & (me_d < last)

    @pl.when(owns_proj)
    def _():
        proj_r[me_d] = projgrad[proj_rows(me_d), :]
        dp_wait(proj_r, N_DP - 1, None, pr)
        out = total(proj_r, N_DP).astype(BF16)
        proj_mine[...] = out
        proj_all[me_d] = out
        peers(lambda t, peer: proj_all_copy(peer).start())

    @pl.when(owns_small)
    def _():
        small_r[me_d] = small[small_rows(me_d), :]
        dp_wait(small_r, N_DP - 1, None, sr)
        out = total(small_r, N_DP)
        small_mine[...] = out
        small_all[me_d - first] = out
        peers(lambda t, peer: small_all_copy(peer).start())

    x_dcap.wait_recv()
    d_caption = 7.0 * total(dcap_r, N_DP)
    gtext_out[...] = text_scale * (
        d_caption - text_f * jnp.sum(text_f * d_caption, axis=1, keepdims=True)
    )

    for ex in (x_text, x_norm, x_part, x_img, x_col, x_row, x_dimg, x_dcap, x_demb, x_dn):
        ex.wait_send()
    wait_blocks("fsdp", N_FSDP, me_f, held, PAIRS, near_s, None)
    wait_blocks("fsdp", N_FSDP, me_f, held, PAIRS - 1, far_s.at[0], None)
    wait_blocks("fsdp", N_FSDP, me_f, mate_r, PAIRS, hs, None)
    wait_blocks("fsdp", N_FSDP, me_f, chip_r, PAIRS - 1, far_s.at[1], None)

    @pl.when(owns_proj)
    def _():
        dp_wait(proj_r, PROJ_OWNERS - 1, ps, None)
        dp_wait(proj_all, PROJ_OWNERS - 1, None, gr.at[0])

    @pl.when(me_d >= first)
    def _():
        dp_wait(proj_r, PROJ_OWNERS, ps, None)
        dp_wait(proj_all, PROJ_OWNERS, None, gr.at[0])

    for k in range(PROJ_OWNERS):
        proj_out[8 * k : 8 * (k + 1), :] = proj_all[k].astype(F32)

    @pl.when(owns_small)
    def _():
        dp_wait(small_r, SMALL_OWNERS - 1, ss, None)
        dp_wait(small_all, SMALL_OWNERS - 1, None, gr.at[1])
        dp_wait(small_r, N_DP - 1, gs.at[1], None)

    @pl.when((me_d < first) | (me_d >= last))
    def _():
        dp_wait(small_r, SMALL_OWNERS, ss, None)
        dp_wait(small_all, SMALL_OWNERS, None, gr.at[1])

    for k in range(BIAS_ROW // 8):
        taps_out[8 * k : 8 * (k + 1), :] = small_all[k]
    rest = small_all[BIAS_ROW // 8]
    taps_out[BIAS_ROW - 1 :, :] = rest[:1]
    bias_out[...] = rest[BIAS_ROW - 48 : BIAS_ROW - 47]
    block_out[...] = rest[BLOCK_ROW - 48 : BLOCK_ROW - 47]
    head_out[...] = rest[HEAD_ROW - 48 : HEAD_ROW - 47]
    loss_out[...] = rest[LOSS_ROW - 48 : LOSS_ROW - 47, :128]

    @pl.when(owns_proj)
    def _():
        wait_blocks("dp", N_DP, me_d, proj_all, N_DP - 1, gs.at[0], None)


def store_kernel(*refs):
    count = (len(refs) - 1) // 2
    copies = [
        pltpu.make_async_copy(refs[n], refs[count + n], refs[-1].at[n]) for n in range(count)
    ]
    for copy in copies:
        copy.start()
    for copy in copies:
        copy.wait()


def dma(*shape):
    return pltpu.SemaphoreType.DMA(shape)


def local(images, dw_weight, dw_bias, block_gain, head_gain, projection, text):
    V = pltpu.VMEM
    maps = (IMGS, MAP_SIDE, MAP_SIDE, CHANNELS)
    lanes = (IMGS, MAP_SIDE, MAP_SIDE, 128)
    wide = (IMGS, CHANNELS)
    two = (IMGS, EMBED)

    def f_blocks(shape, kind):
        return V((N_FSDP,) + shape, kind)

    def d_blocks(shape, kind):
        return V((N_DP,) + shape, kind)

    inputs = (images, dw_weight, dw_bias[None], block_gain[None], head_gain[None], projection, text)
    inputs = [pltpu.with_memory_space_constraint(value, pltpu.HBM) for value in inputs]
    row = (1, SHARD)
    outs = [
        jax.ShapeDtypeStruct(shape, kind)
        for shape, kind in (
            (maps, BF16), ((KERNEL * KERNEL, SHARD), F32), (row, F32), (row, F32), (row, F32),
            ((1, 128), F32), ((SHARD, EMBED), F32), (two, F32),
        )
    ]
    results = pl.pallas_call(
        step_kernel,
        out_shape=outs,
        in_specs=[pl.BlockSpec(memory_space=pltpu.HBM)] * len(inputs),
        out_specs=[VMEM_SPEC] * len(outs),
        scratch_shapes=[
            V(maps, BF16), V((KERNEL * KERNEL, SHARD), F32), V((1, SHARD), F32), V((1, SHARD), F32),
            V((1, SHARD), F32), V((SHARD, EMBED), BF16), V(two, BF16),
            V((ROWS, SHARD), F32), f_blocks((ROWS, SHARD), F32), V((ROWS, CHANNELS), F32),
            V(maps, F32), V(lanes, F32), V(wide, F32), V(lanes, F32),
            V((IMGS, MAP_SIDE, CHANNELS), F32), V(wide, F32),
            f_blocks((IMGS, SHARD), F32), f_blocks((IMGS, SHARD), F32),
            f_blocks(two, F32), f_blocks(two, F32),
            V(two, BF16), f_blocks(two, BF16),
            V((1, 128), F32), f_blocks((1, 128), F32),
            f_blocks(two, F32), f_blocks(two, F32),
            V(two, BF16), f_blocks(two, BF16),
            f_blocks((IMGS, SHARD), F32), f_blocks((IMGS, SHARD), F32),
            V(two, BF16), d_blocks(two, BF16),
            V((1, 128), F32), d_blocks((1, 128), F32),
            d_blocks(two, F32), d_blocks(two, F32),
            V(wide, F32), V((SHARD, EMBED), F32), V((ROWS, CHANNELS), F32), V(wide, F32),
            V(wide, F32), V((IMGS, 128), F32), f_blocks((ROWS, SHARD), F32),
            V((PAIRS, ROWS, SHARD), F32), V((PAIRS, ROWS, SHARD), F32), V((PAIRS, ROWS, SHARD), F32),
            V((ROWS, SHARD), F32), d_blocks((8, EMBED), F32), d_blocks((8, SHARD), F32),
            V((8, EMBED), BF16), V((8, SHARD), F32),
            d_blocks((8, EMBED), BF16), V((SMALL_OWNERS, 8, SHARD), F32),
            dma(7), dma(7), dma(7), dma(3), dma(3), dma(), dma(), dma(), dma(), dma(2), dma(2),
            dma(), dma(PAIRS), dma(), dma(PAIRS), dma(2), dma(2, PAIRS),
        ],
        compiler_params=pltpu.CompilerParams(
            vmem_limit_bytes=48 * 1024 * 1024, collective_id=0, has_side_effects=True
        ),
    )(*inputs)
    grad_images, taps, bias, block, head, loss, sum_proj, grad_text = pl.pallas_call(
        store_kernel,
        out_shape=outs,
        in_specs=[VMEM_SPEC] * len(outs),
        out_specs=[pl.BlockSpec(memory_space=pltpu.HBM)] * len(outs),
        scratch_shapes=[dma(len(outs))],
        compiler_params=pltpu.CompilerParams(vmem_limit_bytes=1024 * 1024),
    )(*results)
    return (loss[0, 0], grad_images, taps, bias[0], block[0], head[0], sum_proj, grad_text)


def solution(mesh):
    return jax.shard_map(
        local,
        mesh=mesh,
        in_specs=(
            P(("dp", "fsdp"), None, None, None),
            P(None, "fsdp"),
            P("fsdp"),
            P("fsdp"),
            P("fsdp"),
            P("fsdp", None),
            P(("dp", "fsdp"), None),
        ),
        out_specs=(
            P(),
            P(("dp", "fsdp"), None, None, None),
            P(None, "fsdp"),
            P("fsdp"),
            P("fsdp"),
            P("fsdp"),
            P("fsdp", None),
            P(("dp", "fsdp"), None),
        ),
        check_vma=False,
    )
```

```python
import jax
import jax.numpy as jnp
from jax import lax
from jax.experimental import pallas as pl
from jax.experimental.pallas import tpu as pltpu
from jax.sharding import PartitionSpec as P

KERNEL = 7
MAP_SIDE = 8
LOGIT_SCALE = 14.0
EPSILON = 1e-06
MESH = pl.DeviceIdType.MESH
F32 = jnp.float32
BF16 = jnp.bfloat16
N_DP = 32
N_FSDP = 16
IMGS = 2
CHANNELS = 3072
SHARD = 192
EMBED = 512
ROWS = 56
BIAS_ROW, BLOCK_ROW, HEAD_ROW, LOSS_ROW = 49, 50, 51, 52
BLOCKS = CHANNELS // 128
VMEM_SPEC = pl.BlockSpec(memory_space=pltpu.VMEM)


def contract(left, right, left_dim, right_dim):
    return lax.dot_general(
        left, right, (((left_dim,), (right_dim,)), ((), ())), preferred_element_type=F32
    )


def copy_to(axis, peer, src, dst, send_sem, recv_sem):
    return pltpu.make_async_remote_copy(
        src_ref=src,
        dst_ref=dst,
        send_sem=send_sem,
        recv_sem=recv_sem,
        device_id={axis: peer},
        device_id_type=MESH,
    )


def loop(low, high, body):
    def step(t, carry):
        body(t)
        return carry

    lax.fori_loop(low, high, step, 0)


def greet(me_f, me_d):
    barrier = pltpu.get_barrier_semaphore()

    def signal(axis, me, count):
        def body(t):
            peer = lax.rem(me + t, count)
            pl.semaphore_signal(barrier, inc=1, device_id={axis: peer}, device_id_type=MESH)

        loop(1, count, body)

    signal("dp", me_d, N_DP)
    signal("fsdp", me_f, N_FSDP)


def greeted():
    pl.semaphore_wait(pltpu.get_barrier_semaphore(), N_FSDP + N_DP - 2)


class Exchange:
    def __init__(self, axis, count, me, source, dst, send_sem, recv_sem):
        self.axis, self.count, self.me = axis, count, me
        self.source, self.dst, self.send_sem, self.recv_sem = source, dst, send_sem, recv_sem

    def start(self):
        def body(t):
            offset = 1 + lax.rem(t + self.count // 2 - 2, self.count - 1)
            peer = lax.rem(self.me + offset, self.count)
            copy_to(
                self.axis, peer, self.source(peer), self.dst.at[self.me], self.send_sem, self.recv_sem
            ).start()

        loop(0, self.count - 1, body)

    def wait_recv(self):
        wait_blocks(self.axis, self.count, self.me, self.dst, self.count - 1, None, self.recv_sem)

    def wait_send(self):
        wait_blocks(self.axis, self.count, self.me, self.dst, self.count - 1, self.send_sem, None)


def wait_blocks(axis, count, me, like, blocks, send_sem, recv_sem):
    window = like.at[pl.ds(0, blocks)]
    sem = recv_sem if send_sem is None else send_sem
    copy = copy_to(axis, lax.rem(me + 1, count), window, window, sem, sem)
    if send_sem is None:
        copy.wait_recv()
    else:
        copy.wait_send()


def join_pairs(read, write):
    for p in range(N_FSDP // 2):
        write(p, jnp.concatenate([read(2 * p), read(2 * p + 1)], axis=1))


def shifted(value, amount):
    if amount == 0:
        return value
    place = lax.broadcasted_iota(jnp.int32, value.shape, 0)
    rolled = pltpu.roll(value, amount % MAP_SIDE, 0)
    inside = place >= amount if amount > 0 else place < MAP_SIDE + amount
    return jnp.where(inside, rolled, 0.0)


def lanes_of(block):
    return pl.ds(pl.multiple_of(block * 128, 128), 128)


PAIRS = N_FSDP // 2
PROJ_OWNERS = SHARD // 8
SMALL_OWNERS = ROWS // 8


def pair_lanes(p):
    return pl.ds(pl.multiple_of(p * (2 * SHARD), 128), 2 * SHARD)


DENSE, TAKEN = 40, KERNEL * KERNEL + 2


def dense(rows):
    rest = rows[DENSE:]
    spare = [rest[:, 64 * n : 64 * (n + 1)] for n in range(3)]
    spare.append(jnp.zeros((DENSE - 3 * (TAKEN - DENSE), 64), F32))
    return jnp.concatenate([rows[:DENSE], jnp.concatenate(spare, axis=0)], axis=1)


def rest_of(block):
    count = TAKEN - DENSE
    spare = block[:, SHARD:]
    return jnp.concatenate([spare[count * n : count * (n + 1)] for n in range(3)], axis=1)


def stack(ref, count):
    return jnp.concatenate([ref[k] for k in range(count)], axis=0)


def total(ref, count):
    out = ref[0]
    for k in range(1, count):
        out = out + ref[k]
    return out


def spread(ref, value):
    for k in range(ref.shape[0]):
        ref[k] = value[IMGS * k : IMGS * (k + 1)]


def forward_block(block, images, full, z, sums, isum):
    margin = KERNEL // 2
    lanes = lanes_of(block)
    for b in range(IMGS):
        rows = [images[b, i, :, lanes].astype(F32) for i in range(MAP_SIDE)]
        pixels = rows[0]
        for i in range(1, MAP_SIDE):
            pixels = pixels + rows[i]
        isum[b, :, lanes] = pixels
        bias = jnp.broadcast_to(full[pl.ds(BIAS_ROW, 1), lanes], (MAP_SIDE, 128))
        acc = [bias] * MAP_SIDE
        for s in range(KERNEL):
            cols = [shifted(row, margin - s) for row in rows]
            for r in range(KERNEL):
                tap = jnp.broadcast_to(full[pl.ds(r * KERNEL + s, 1), lanes], (MAP_SIDE, 128))
                for i in range(MAP_SIDE):
                    if 0 <= i + r - margin < MAP_SIDE:
                        acc[i] = acc[i] + cols[i + r - margin] * tap
        for i in range(MAP_SIDE):
            z[b, i, :, lanes] = acc[i]
            sums[b, i] += acc[i]


def forward_norm(full, z, inv, zsum, sums, isum, pooled):
    mean = jnp.sum(sums[...], axis=3, keepdims=True) * (1.0 / CHANNELS)
    inv[...] = jnp.broadcast_to(mean, sums.shape)
    sums[...] = jnp.zeros_like(sums)

    def centre(block):
        lanes = lanes_of(block)
        value = z[:, :, :, lanes] - inv[...]
        z[:, :, :, lanes] = value
        sums[...] += value * value

    loop(0, BLOCKS, centre)
    var = jnp.sum(sums[...], axis=3, keepdims=True) * (1.0 / CHANNELS)
    inv[...] = jnp.broadcast_to(lax.rsqrt(var + EPSILON), sums.shape)

    def norm(block):
        lanes = lanes_of(block)
        value = z[:, :, :, lanes] * inv[...]
        z[:, :, :, lanes] = value
        zs = jnp.sum(jnp.sum(value, axis=1), axis=1)
        zsum[:, lanes] = zs
        gain = full[pl.ds(BLOCK_ROW, 1), lanes]
        img = jnp.sum(isum[:, :, lanes], axis=1)
        pooled[:, lanes] = (img + zs * gain) * (1.0 / (MAP_SIDE * MAP_SIDE))

    loop(0, BLOCKS, norm)
    value = pooled[...]
    centred = value - jnp.mean(value, axis=1, keepdims=True)
    inverse = lax.rsqrt(jnp.mean(centred * centred, axis=1, keepdims=True) + EPSILON)
    return centred * inverse, inverse


def backward_block(block, images, z, inv, full, dh, dn, sums, mean1, grads, gimg):
    margin = KERNEL // 2
    lanes = lanes_of(block)
    maps, pixels, acc = [], [], []
    bias = None
    for b in range(IMGS):
        row = jnp.broadcast_to(dn[pl.ds(b, 1), lanes], (MAP_SIDE, 128)) - jnp.broadcast_to(
            mean1[pl.ds(b, 1), :], (MAP_SIDE, 128)
        )
        hidden = jnp.broadcast_to(dh[pl.ds(b, 1), lanes], (MAP_SIDE, 128))
        for i in range(MAP_SIDE):
            value = inv[b, i] * (row - z[b, i, :, lanes] * sums[b, i])
            maps.append(value)
            bias = value if bias is None else bias + value
            pixels.append(images[b, i, :, lanes].astype(F32))
            acc.append(hidden)
    grads[pl.ds(BIAS_ROW, 1), lanes] = jnp.sum(bias, axis=0, keepdims=True)
    for s in range(KERNEL):
        grad = [None] * KERNEL
        for b in range(IMGS):
            own = range(b * MAP_SIDE, (b + 1) * MAP_SIDE)
            cols = [shifted(maps[k], s - margin) for k in own]
            for r in range(KERNEL):
                tap = jnp.broadcast_to(full[pl.ds(r * KERNEL + s, 1), lanes], (MAP_SIDE, 128))
                for i in range(MAP_SIDE):
                    if 0 <= i - r + margin < MAP_SIDE:
                        col = cols[i - r + margin]
                        k = own[i]
                        acc[k] = acc[k] + col * tap
                        term = col * pixels[k]
                        grad[r] = term if grad[r] is None else grad[r] + term
        for r in range(KERNEL):
            grads[pl.ds(r * KERNEL + s, 1), lanes] = jnp.sum(grad[r], axis=0, keepdims=True)
    for b in range(IMGS):
        for i in range(MAP_SIDE):
            gimg[b, i, :, lanes] = acc[b * MAP_SIDE + i].astype(BF16)


def step_kernel(
    images_hbm, w_hbm, bias_hbm, gain_hbm, head_hbm, proj_hbm, text_hbm,
    gimg, taps_out, bias_out, block_out, head_out, loss_out, proj_out, gtext_out,
    images, w_in, bias_in, gain_in, head_in, proj_in, text_in,
    pack, held, full, z, inv, zsum, sums, isum, pooled,
    normed_s, normed_r, part_s, part_r, img_s, img_r, row_s, row_r, dimg_s, dimg_r,
    demb_s, demb_r, dn_s, dn_r, text_s, text_r, col_s, col_r, dcap_s, dcap_r,
    dnormed, projgrad, grads, dh, dn, mean1, blocks_s, mate_r, chip_s, chip_r,
    small, proj_r, small_r, proj_mine, small_mine, proj_all, small_all,
    load_sem, fs, fr, ds, dr, ps, pr, ss, sr, gs, gr, hs, hr, near_s, near_r, far_s, far_r,
):
    me_f, me_d = lax.axis_index("fsdp"), lax.axis_index("dp")
    my_pair, core = lax.div(me_f, 2), lax.rem(me_f, 2)
    mate = 2 * my_pair + 1 - core
    greet(me_f, me_d)
    loads = [
        pltpu.make_async_copy(src, dst, load_sem.at[n])
        for n, (src, dst) in enumerate(
            (
                (w_hbm, w_in), (bias_hbm, bias_in), (gain_hbm, gain_in), (text_hbm, text_in),
                (images_hbm, images), (head_hbm, head_in), (proj_hbm, proj_in),
            )
        )
    ]
    for load in loads:
        load.start()

    def fex(n, source, dst):
        return Exchange("fsdp", N_FSDP, me_f, source, dst, fs.at[n], fr.at[n])

    def dex(n, source, dst):
        return Exchange("dp", N_DP, me_d, source, dst, ds.at[n], dr.at[n])

    sums[...] = jnp.zeros_like(sums)
    for load in loads[:4]:
        load.wait()
    rows = dense(jnp.concatenate([w_in[...], bias_in[...], gain_in[...]], axis=0))
    pack[...] = rows
    held[me_f] = rows
    text = text_in[...].astype(F32)
    text_scale = lax.rsqrt(jnp.sum(text * text, axis=1, keepdims=True) + EPSILON)
    text_f = text * text_scale
    text_unit = text_f.astype(BF16)
    text_s[...] = text_unit
    text_r[me_d] = text_unit
    greeted()

    def near_copy(p, block, dst):
        return copy_to("fsdp", mate, block, dst, near_s, near_r.at[p])

    def far_copy(t, n, block, dst):
        q = lax.rem(my_pair + t, PAIRS)
        return copy_to("fsdp", 2 * q + core, block, dst, far_s.at[n], far_r.at[n, my_pair])

    near_copy(my_pair, pack, held.at[me_f]).start()
    loop(1, PAIRS, lambda t: far_copy(t, 0, pack, held.at[me_f]).start())
    x_text = dex(0, lambda peer: text_s, text_r)
    x_text.start()
    for load in loads[4:]:
        load.wait()

    def hand_on(t):
        p = lax.rem(my_pair - t + PAIRS, PAIRS)
        block = held.at[2 * p + core]
        copy_to("fsdp", 2 * p + core, block, block, far_s.at[0], far_r.at[0, p]).wait_recv()
        near_copy(p, block, block).start()

    def forward_pair(t):
        p = lax.rem(my_pair - t + PAIRS, PAIRS)
        block = held.at[2 * p + 1 - core]
        near_copy(p, block, block).wait_recv()
        left, right = held[2 * p], held[2 * p + 1]
        full[:DENSE, pair_lanes(p)] = jnp.concatenate([left[:, :SHARD], right[:, :SHARD]], axis=1)
        full[DENSE:TAKEN, pair_lanes(p)] = jnp.concatenate([rest_of(left), rest_of(right)], axis=1)
        loop(0, 3, lambda k: forward_block(3 * p + k, images, full, z, sums, isum))

        @pl.when(t == 0)
        def _():
            hand_on(1)

        @pl.when(t + 2 < PAIRS)
        def _():
            hand_on(t + 2)

    loop(0, PAIRS, forward_pair)
    pool_normed, pool_inverse = forward_norm(full, z, inv, zsum, sums, isum, pooled)

    for p in range(PAIRS):
        value = pool_normed[:, 384 * p : 384 * (p + 1)]
        normed_s[2 * p] = value[:, :SHARD]
        normed_s[2 * p + 1] = value[:, SHARD:]
    pooled[...] = pool_normed
    normed_r[me_f] = normed_s[me_f]
    x_norm = fex(0, lambda peer: normed_s.at[peer], normed_r)
    x_norm.start()
    x_text.wait_recv()
    text_cols = stack(text_r, N_DP)
    x_norm.wait_recv()
    normed = stack(normed_r, N_FSDP)
    head = head_in[...]
    query = (normed * head).astype(BF16)
    part = jnp.dot(query, proj_in[...], preferred_element_type=F32)
    spread(part_s, part)
    part_r[me_f] = part_s[me_f]
    x_part = fex(1, lambda peer: part_s.at[peer], part_r)
    x_part.start()
    x_part.wait_recv()
    embedding = total(part_r, N_FSDP)
    image_scale = lax.rsqrt(jnp.sum(embedding * embedding, axis=1, keepdims=True) + EPSILON)
    image_f = embedding * image_scale
    image_unit = image_f.astype(BF16)
    img_s[...] = image_unit
    img_r[me_f] = image_unit
    x_img = fex(2, lambda peer: img_s, img_r)
    x_img.start()
    diagonal = LOGIT_SCALE * jnp.sum(image_unit.astype(F32) * text_unit.astype(F32))

    n_row, n_col = N_FSDP * IMGS, N_DP * IMGS
    eye = (
        lax.broadcasted_iota(jnp.int32, (n_row, 128), 0)
        == lax.broadcasted_iota(jnp.int32, (n_row, 128), 1)
    )
    x_img.wait_recv()
    image_rows = stack(img_r, N_FSDP)
    logits = LOGIT_SCALE * contract(image_rows, text_cols, 1, 1)
    exps = jnp.exp(logits)
    col_part = jnp.sum(exps, axis=0, keepdims=True)
    col_flat = jnp.concatenate([col_part, jnp.zeros((1, 128 - n_col), F32)], axis=1)
    col_s[...] = col_flat
    col_r[me_d] = col_flat
    x_col = dex(1, lambda peer: col_s, col_r)
    x_col.start()
    row_part = jnp.sum(exps, axis=1, keepdims=True)
    row_flat = jnp.sum(jnp.where(eye, row_part, 0.0), axis=0, keepdims=True)
    row_s[...] = row_flat
    row_r[me_f] = row_flat
    x_row = fex(3, lambda peer: row_s, row_r)
    x_row.start()
    x_row.wait_recv()
    row_sum = total(row_r, N_FSDP)
    row_lse = jnp.log(jnp.sum(jnp.where(eye, row_sum, 0.0), axis=1, keepdims=True))
    row_term = jnp.exp(logits - row_lse)
    at_row = lax.broadcasted_iota(jnp.int32, (n_row, n_col), 0)
    at_col = lax.broadcasted_iota(jnp.int32, (n_row, n_col), 1)
    pair = jnp.where(
        (at_row - IMGS * me_f == at_col - IMGS * me_d)
        & (at_row >= IMGS * me_f)
        & (at_row < IMGS * me_f + IMGS),
        2.0,
        0.0,
    )
    x_col.wait_recv()
    col_lse = jnp.log(total(col_r, N_DP)[:, :n_col])
    weights = (row_term + jnp.exp(logits - col_lse) - pair).astype(BF16)
    dimg = jnp.dot(weights, text_cols, preferred_element_type=F32)
    spread(dimg_s, dimg)
    dimg_r[me_f] = dimg_s[me_f]
    x_dimg = fex(4, lambda peer: dimg_s.at[peer], dimg_r)
    x_dimg.start()
    dcap = contract(weights, image_rows, 0, 0)
    spread(dcap_s, dcap)
    dcap_r[me_d] = dcap_s[me_d]
    x_dcap = dex(2, lambda peer: dcap_s.at[peer], dcap_r)
    x_dcap.start()
    loss_part = (
        jnp.sum(row_lse) * (1.0 / N_FSDP) + jnp.sum(col_lse) * (1.0 / N_DP) - 2.0 * diagonal
    )
    x_dimg.wait_recv()
    d_image = 7.0 * total(dimg_r, N_FSDP)
    d_embedding = (
        image_scale * (d_image - image_f * jnp.sum(image_f * d_image, axis=1, keepdims=True))
    ).astype(BF16)
    demb_s[...] = d_embedding
    demb_r[me_f] = d_embedding
    x_demb = fex(5, lambda peer: demb_s, demb_r)
    x_demb.start()
    x_demb.wait_recv()
    demb = stack(demb_r, N_FSDP)
    d_query = contract(demb, proj_in[...], 1, 1)
    spread(dn_s, d_query * head)
    dn_r[me_f] = dn_s[me_f]
    x_dn = fex(6, lambda peer: dn_s.at[peer], dn_r)
    x_dn.start()
    head_grad = jnp.sum(d_query * normed, axis=0, keepdims=True)
    projgrad[...] = contract(query, demb, 0, 0)

    first = PROJ_OWNERS
    last = PROJ_OWNERS + SMALL_OWNERS

    def proj_rows(k):
        return pl.ds(pl.multiple_of(k * 8, 8), 8)

    def small_rows(k):
        return pl.ds(pl.multiple_of((k - first) * 8, 8), 8)

    def peers(act):
        def body(t):
            act(t, lax.rem(me_d + 1 + lax.rem(t + 11, N_DP - 1), N_DP))

        loop(0, N_DP - 1, body)

    def proj_copy(t, peer, to):
        return copy_to("dp", peer, projgrad.at[proj_rows(to)], proj_r.at[me_d], ps, pr)

    def small_copy(t, peer, to):
        return copy_to("dp", peer, small.at[small_rows(to)], small_r.at[me_d], ss, sr)

    def start_proj(t, peer):
        @pl.when(peer < first)
        def _():
            proj_copy(t, peer, peer).start()

    peers(start_proj)

    x_dn.wait_recv()

    def write(p, value):
        dnormed[:, 384 * p : 384 * (p + 1)] = value

    join_pairs(lambda k: dn_r[k], write)

    normed = pooled[...]
    d_normed = dnormed[...]
    d_pooled = pool_inverse * (
        d_normed
        - jnp.mean(d_normed, axis=1, keepdims=True)
        - normed * jnp.mean(d_normed * normed, axis=1, keepdims=True)
    )
    d_hidden = d_pooled * (1.0 / (MAP_SIDE * MAP_SIDE))
    dh[...] = d_hidden
    d_norm = d_hidden * full[BLOCK_ROW : BLOCK_ROW + 1, :]
    dn[...] = d_norm
    grads[ROWS - 8 :, :] = jnp.zeros((8, CHANNELS), F32)
    grads[BLOCK_ROW : BLOCK_ROW + 1, :] = jnp.sum(d_hidden * zsum[...], axis=0, keepdims=True)
    grads[LOSS_ROW : LOSS_ROW + 1, :] = jnp.full(
        (1, CHANNELS), loss_part * (0.5 / (N_DP * N_FSDP * IMGS)), F32
    )
    mean1[...] = jnp.broadcast_to(jnp.mean(d_norm, axis=1, keepdims=True), mean1.shape)
    sums[...] = jnp.zeros_like(sums)

    def project(block):
        lanes = lanes_of(block)
        for b in range(IMGS):
            row = jnp.broadcast_to(dn[pl.ds(b, 1), lanes], (MAP_SIDE, 128))
            for i in range(MAP_SIDE):
                sums[b, i] += row * z[b, i, :, lanes]

    loop(0, BLOCKS, project)
    mean2 = jnp.sum(sums[...], axis=3, keepdims=True) * (1.0 / CHANNELS)
    sums[...] = jnp.broadcast_to(mean2, sums.shape)

    owns_proj = me_d < first

    def dp_wait(like, blocks, send_sem, recv_sem):
        wait_blocks("dp", N_DP, me_d, like, blocks, send_sem, recv_sem)

    my_z, my_x = lax.div(me_d, 2), lax.rem(me_d, 2)
    n_z = N_DP // 2
    z_owners = PROJ_OWNERS // 2

    def proj_start():
        def body(t):
            offset = 1 + lax.rem(t + n_z // 2 - 3, n_z - 1)
            to = 2 * lax.rem(my_z + offset, n_z) + my_x
            copy_to("dp", to, proj_mine, proj_all.at[my_x, my_z], gs.at[0], gr.at[0]).start()

        loop(0, n_z - 1, body)

    def proj_window(x, blocks):
        return proj_all.at[x, pl.ds(0, blocks)]

    def proj_wait(x, blocks, send_sem, recv_sem):
        window = proj_window(x, blocks)
        sem = recv_sem if send_sem is None else send_sem
        copy = copy_to("dp", me_d + 1 - 2 * my_x, window, window, sem, sem)
        if send_sem is None:
            copy.wait_recv()
        else:
            copy.wait_send()

    def proj_hand_on():
        window = proj_window(my_x, z_owners)
        return copy_to("dp", me_d + 1 - 2 * my_x, window, window, gs.at[2], gr.at[2])

    def sum_proj():
        proj_r[me_d] = projgrad[proj_rows(me_d), :]
        dp_wait(proj_r, N_DP - 1, None, pr)
        out = total(proj_r, N_DP).astype(BF16)
        proj_mine[...] = out
        proj_all[my_x, my_z] = out
        proj_start()

    def mate_copy(p):
        return copy_to(
            "fsdp", mate, blocks_s.at[2 * p + 1 - core], mate_r.at[p], hs, hr.at[p]
        )

    def chip_sum(p):
        copy_to("fsdp", mate, mate_r.at[p], mate_r.at[p], hs, hr.at[p]).wait_recv()
        return blocks_s[2 * p + core] + mate_r[p]

    def backward_order(t):
        y, x = lax.div(my_pair, 2), lax.rem(my_pair, 2)
        return 2 * lax.rem(y + 1 + lax.div(t - 1, 2), PAIRS // 2) + lax.rem(x + t, 2)

    def send_chip(t):
        p = backward_order(t)
        chip_s[p] = chip_sum(p)
        copy_to(
            "fsdp", 2 * p + core, chip_s.at[p], chip_r.at[my_pair], far_s.at[1], far_r.at[1, my_pair]
        ).start()

    def backward_pair(t):
        p = backward_order(t)

        def piece(k):
            backward_block(3 * p + k, images, z, inv, full, dh, dn, sums, mean1, grads, gimg)

            @pl.when((k == 0) & (t > 1))
            def _():
                send_chip(t - 1)

        loop(0, 3, piece)
        value = grads[:, pair_lanes(p)]
        blocks_s[2 * p] = value[:, :SHARD]
        blocks_s[2 * p + 1] = value[:, SHARD:]
        mate_copy(p).start()

    loop(1, PAIRS + 1, backward_pair)
    chip_r[my_pair] = chip_sum(my_pair)

    def chip_wait(t):
        p = lax.rem(my_pair + t, PAIRS)
        copy_to(
            "fsdp", 2 * p + core, chip_r.at[p], chip_r.at[p], far_s.at[1], far_r.at[1, p]
        ).wait_recv()

    loop(1, PAIRS, chip_wait)
    small[...] = total(chip_r, PAIRS)
    small[HEAD_ROW : HEAD_ROW + 1, :] = head_grad

    def start_small(t, peer):
        @pl.when((peer >= first) & (peer < last))
        def _():
            small_copy(t, peer, peer).start()

    peers(start_small)

    def small_all_copy(peer):
        return copy_to("dp", peer, small_mine, small_all.at[me_d - first], gs.at[1], gr.at[1])

    @pl.when(owns_proj)
    def _():
        sum_proj()

    owns_small = (me_d >= first) & (me_d < last)

    @pl.when(owns_small)
    def _():
        small_r[me_d] = small[small_rows(me_d), :]
        dp_wait(small_r, N_DP - 1, None, sr)
        out = total(small_r, N_DP)
        small_mine[...] = out
        small_all[me_d - first] = out
        peers(lambda t, peer: small_all_copy(peer).start())

    x_dcap.wait_recv()
    d_caption = 7.0 * total(dcap_r, N_DP)
    gtext_out[...] = text_scale * (
        d_caption - text_f * jnp.sum(text_f * d_caption, axis=1, keepdims=True)
    )

    for ex in (x_text, x_norm, x_part, x_img, x_col, x_row, x_dimg, x_dcap, x_demb, x_dn):
        ex.wait_send()
    wait_blocks("fsdp", N_FSDP, me_f, held, PAIRS, near_s, None)
    wait_blocks("fsdp", N_FSDP, me_f, held, PAIRS - 1, far_s.at[0], None)
    wait_blocks("fsdp", N_FSDP, me_f, mate_r, PAIRS, hs, None)
    wait_blocks("fsdp", N_FSDP, me_f, chip_r, PAIRS - 1, far_s.at[1], None)

    @pl.when(owns_proj)
    def _():
        dp_wait(proj_r, PROJ_OWNERS - 1, ps, None)
        proj_wait(my_x, z_owners - 1, None, gr.at[0])

    @pl.when(me_d >= first)
    def _():
        dp_wait(proj_r, PROJ_OWNERS, ps, None)
        proj_wait(my_x, z_owners, None, gr.at[0])

    handed = proj_hand_on()
    handed.start()

    @pl.when(owns_small)
    def _():
        dp_wait(small_r, SMALL_OWNERS - 1, ss, None)
        dp_wait(small_all, SMALL_OWNERS - 1, None, gr.at[1])
        dp_wait(small_r, N_DP - 1, gs.at[1], None)

    @pl.when((me_d < first) | (me_d >= last))
    def _():
        dp_wait(small_r, SMALL_OWNERS, ss, None)
        dp_wait(small_all, SMALL_OWNERS, None, gr.at[1])

    for k in range(BIAS_ROW // 8):
        taps_out[8 * k : 8 * (k + 1), :] = small_all[k]
    rest = small_all[BIAS_ROW // 8]
    taps_out[BIAS_ROW - 1 :, :] = rest[:1]
    bias_out[...] = rest[BIAS_ROW - 48 : BIAS_ROW - 47]
    block_out[...] = rest[BLOCK_ROW - 48 : BLOCK_ROW - 47]
    head_out[...] = rest[HEAD_ROW - 48 : HEAD_ROW - 47]
    loss_out[...] = rest[LOSS_ROW - 48 : LOSS_ROW - 47, :128]

    @pl.when(owns_proj)
    def _():
        proj_wait(0, n_z - 1, gs.at[0], None)

    proj_wait(1 - my_x, z_owners, None, gr.at[2])
    for k in range(PROJ_OWNERS):
        proj_out[8 * k : 8 * (k + 1), :] = proj_all[k % 2, k // 2].astype(F32)
    handed.wait_send()


def store_kernel(*refs):
    count = (len(refs) - 1) // 2
    copies = [
        pltpu.make_async_copy(refs[n], refs[count + n], refs[-1].at[n]) for n in range(count)
    ]
    for copy in copies:
        copy.start()
    for copy in copies:
        copy.wait()


def dma(*shape):
    return pltpu.SemaphoreType.DMA(shape)


def local(images, dw_weight, dw_bias, block_gain, head_gain, projection, text):
    V = pltpu.VMEM
    maps = (IMGS, MAP_SIDE, MAP_SIDE, CHANNELS)
    lanes = (IMGS, MAP_SIDE, MAP_SIDE, 128)
    wide = (IMGS, CHANNELS)
    two = (IMGS, EMBED)

    def f_blocks(shape, kind):
        return V((N_FSDP,) + shape, kind)

    def d_blocks(shape, kind):
        return V((N_DP,) + shape, kind)

    inputs = (images, dw_weight, dw_bias[None], block_gain[None], head_gain[None], projection, text)
    inputs = [pltpu.with_memory_space_constraint(value, pltpu.HBM) for value in inputs]
    row = (1, SHARD)
    outs = [
        jax.ShapeDtypeStruct(shape, kind)
        for shape, kind in (
            (maps, BF16), ((KERNEL * KERNEL, SHARD), F32), (row, F32), (row, F32), (row, F32),
            ((1, 128), F32), ((SHARD, EMBED), F32), (two, F32),
        )
    ]
    results = pl.pallas_call(
        step_kernel,
        out_shape=outs,
        in_specs=[pl.BlockSpec(memory_space=pltpu.HBM)] * len(inputs),
        out_specs=[VMEM_SPEC] * len(outs),
        scratch_shapes=[
            V(maps, BF16), V((KERNEL * KERNEL, SHARD), F32), V((1, SHARD), F32), V((1, SHARD), F32),
            V((1, SHARD), F32), V((SHARD, EMBED), BF16), V(two, BF16),
            V((DENSE, 256), F32), f_blocks((DENSE, 256), F32), V((ROWS, CHANNELS), F32),
            V(maps, F32), V(lanes, F32), V(wide, F32), V(lanes, F32),
            V((IMGS, MAP_SIDE, CHANNELS), F32), V(wide, F32),
            f_blocks((IMGS, SHARD), F32), f_blocks((IMGS, SHARD), F32),
            f_blocks(two, F32), f_blocks(two, F32),
            V(two, BF16), f_blocks(two, BF16),
            V((1, 128), F32), f_blocks((1, 128), F32),
            f_blocks(two, F32), f_blocks(two, F32),
            V(two, BF16), f_blocks(two, BF16),
            f_blocks((IMGS, SHARD), F32), f_blocks((IMGS, SHARD), F32),
            V(two, BF16), d_blocks(two, BF16),
            V((1, 128), F32), d_blocks((1, 128), F32),
            d_blocks(two, F32), d_blocks(two, F32),
            V(wide, F32), V((SHARD, EMBED), F32), V((ROWS, CHANNELS), F32), V(wide, F32),
            V(wide, F32), V((IMGS, 128), F32), f_blocks((ROWS, SHARD), F32),
            V((PAIRS, ROWS, SHARD), F32), V((PAIRS, ROWS, SHARD), F32), V((PAIRS, ROWS, SHARD), F32),
            V((ROWS, SHARD), F32), d_blocks((8, EMBED), F32), d_blocks((8, SHARD), F32),
            V((8, EMBED), BF16), V((8, SHARD), F32),
            V((2, N_DP // 2, 8, EMBED), BF16), V((SMALL_OWNERS, 8, SHARD), F32),
            dma(7), dma(7), dma(7), dma(3), dma(3), dma(), dma(), dma(), dma(), dma(3), dma(3),
            dma(), dma(PAIRS), dma(), dma(PAIRS), dma(2), dma(2, PAIRS),
        ],
        compiler_params=pltpu.CompilerParams(
            vmem_limit_bytes=48 * 1024 * 1024, collective_id=0, has_side_effects=True
        ),
    )(*inputs)
    grad_images, taps, bias, block, head, loss, sum_proj, grad_text = pl.pallas_call(
        store_kernel,
        out_shape=outs,
        in_specs=[VMEM_SPEC] * len(outs),
        out_specs=[pl.BlockSpec(memory_space=pltpu.HBM)] * len(outs),
        scratch_shapes=[dma(len(outs))],
        compiler_params=pltpu.CompilerParams(vmem_limit_bytes=1024 * 1024),
    )(*results)
    return (loss[0, 0], grad_images, taps, bias[0], block[0], head[0], sum_proj, grad_text)


def solution(mesh):
    return jax.shard_map(
        local,
        mesh=mesh,
        in_specs=(
            P(("dp", "fsdp"), None, None, None),
            P(None, "fsdp"),
            P("fsdp"),
            P("fsdp"),
            P("fsdp"),
            P("fsdp", None),
            P(("dp", "fsdp"), None),
        ),
        out_specs=(
            P(),
            P(("dp", "fsdp"), None, None, None),
            P(None, "fsdp"),
            P("fsdp"),
            P("fsdp"),
            P("fsdp"),
            P("fsdp", None),
            P(("dp", "fsdp"), None),
        ),
        check_vma=False,
    )
```

```python
import jax
import jax.numpy as jnp
from jax import lax
from jax.experimental import pallas as pl
from jax.experimental.pallas import tpu as pltpu
from jax.sharding import PartitionSpec as P

KERNEL = 7
MAP_SIDE = 8
LOGIT_SCALE = 14.0
EPSILON = 1e-06
MESH = pl.DeviceIdType.MESH
F32 = jnp.float32
BF16 = jnp.bfloat16
N_DP = 32
N_FSDP = 16
IMGS = 2
CHANNELS = 3072
SHARD = 192
EMBED = 512
ROWS = 56
BIAS_ROW, BLOCK_ROW, HEAD_ROW, LOSS_ROW = 49, 50, 51, 52
BLOCKS = CHANNELS // 128
VMEM_SPEC = pl.BlockSpec(memory_space=pltpu.VMEM)


def contract(left, right, left_dim, right_dim):
    return lax.dot_general(
        left, right, (((left_dim,), (right_dim,)), ((), ())), preferred_element_type=F32
    )


def copy_to(axis, peer, src, dst, send_sem, recv_sem):
    return pltpu.make_async_remote_copy(
        src_ref=src,
        dst_ref=dst,
        send_sem=send_sem,
        recv_sem=recv_sem,
        device_id={axis: peer},
        device_id_type=MESH,
    )


def loop(low, high, body):
    def step(t, carry):
        body(t)
        return carry

    lax.fori_loop(low, high, step, 0)


def far_first(count, far, body):
    loop(far, count, body)
    loop(1, far, body)


def greet(me_f, me_d):
    barrier = pltpu.get_barrier_semaphore()

    def signal(axis, me, count):
        def body(t):
            peer = lax.rem(me + t, count)
            pl.semaphore_signal(barrier, inc=1, device_id={axis: peer}, device_id_type=MESH)

        loop(1, count, body)

    signal("dp", me_d, N_DP)
    signal("fsdp", me_f, N_FSDP)


def greeted():
    pl.semaphore_wait(pltpu.get_barrier_semaphore(), N_FSDP + N_DP - 2)


class Exchange:
    def __init__(self, axis, count, me, source, dst, send_sem, recv_sem):
        self.axis, self.count, self.me = axis, count, me
        self.source, self.dst, self.send_sem, self.recv_sem = source, dst, send_sem, recv_sem

    def start(self):
        def body(offset):
            peer = lax.rem(self.me + offset, self.count)
            copy_to(
                self.axis, peer, self.source(peer), self.dst.at[self.me], self.send_sem, self.recv_sem
            ).start()

        far_first(self.count, self.count // 2 - 1, body)

    def wait_recv(self):
        wait_blocks(self.axis, self.count, self.me, self.dst, self.count - 1, None, self.recv_sem)

    def wait_send(self):
        wait_blocks(self.axis, self.count, self.me, self.dst, self.count - 1, self.send_sem, None)


def wait_blocks(axis, count, me, like, blocks, send_sem, recv_sem):
    window = like.at[pl.ds(0, blocks)]
    sem = recv_sem if send_sem is None else send_sem
    copy = copy_to(axis, lax.rem(me + 1, count), window, window, sem, sem)
    if send_sem is None:
        copy.wait_recv()
    else:
        copy.wait_send()


def join_pairs(read, write):
    for p in range(N_FSDP // 2):
        write(p, jnp.concatenate([read(2 * p), read(2 * p + 1)], axis=1))


def shifted(value, amount):
    if amount == 0:
        return value
    place = lax.broadcasted_iota(jnp.int32, value.shape, 0)
    rolled = pltpu.roll(value, amount % MAP_SIDE, 0)
    inside = place >= amount if amount > 0 else place < MAP_SIDE + amount
    return jnp.where(inside, rolled, 0.0)


def lanes_of(block):
    return pl.ds(pl.multiple_of(block * 128, 128), 128)


PAIRS = N_FSDP // 2
PROJ_OWNERS = SHARD // 8
SMALL_OWNERS = ROWS // 8


def pair_lanes(p):
    return pl.ds(pl.multiple_of(p * (2 * SHARD), 128), 2 * SHARD)


DENSE, TAKEN = 40, KERNEL * KERNEL + 2


def dense(rows):
    rest = rows[DENSE:]
    spare = [rest[:, 64 * n : 64 * (n + 1)] for n in range(3)]
    spare.append(jnp.zeros((DENSE - 3 * (TAKEN - DENSE), 64), F32))
    return jnp.concatenate([rows[:DENSE], jnp.concatenate(spare, axis=0)], axis=1)


def rest_of(block):
    count = TAKEN - DENSE
    spare = block[:, SHARD:]
    return jnp.concatenate([spare[count * n : count * (n + 1)] for n in range(3)], axis=1)


def stack(ref, count):
    return jnp.concatenate([ref[k] for k in range(count)], axis=0)


def total(ref, count):
    out = ref[0]
    for k in range(1, count):
        out = out + ref[k]
    return out


def spread(ref, value):
    for k in range(ref.shape[0]):
        ref[k] = value[IMGS * k : IMGS * (k + 1)]


def forward_block(block, images, full, z, sums, isum):
    margin = KERNEL // 2
    lanes = lanes_of(block)
    for b in range(IMGS):
        rows = [images[b, i, :, lanes].astype(F32) for i in range(MAP_SIDE)]
        pixels = rows[0]
        for i in range(1, MAP_SIDE):
            pixels = pixels + rows[i]
        isum[b, :, lanes] = pixels
        bias = jnp.broadcast_to(full[pl.ds(BIAS_ROW, 1), lanes], (MAP_SIDE, 128))
        acc = [bias] * MAP_SIDE
        for s in range(KERNEL):
            cols = [shifted(row, margin - s) for row in rows]
            for r in range(KERNEL):
                tap = jnp.broadcast_to(full[pl.ds(r * KERNEL + s, 1), lanes], (MAP_SIDE, 128))
                for i in range(MAP_SIDE):
                    if 0 <= i + r - margin < MAP_SIDE:
                        acc[i] = acc[i] + cols[i + r - margin] * tap
        for i in range(MAP_SIDE):
            z[b, i, :, lanes] = acc[i]
            sums[b, i] += acc[i]


def forward_norm(full, z, inv, zsum, sums, isum, pooled):
    mean = jnp.sum(sums[...], axis=3, keepdims=True) * (1.0 / CHANNELS)
    inv[...] = jnp.broadcast_to(mean, sums.shape)
    sums[...] = jnp.zeros_like(sums)

    def centre(block):
        lanes = lanes_of(block)
        value = z[:, :, :, lanes] - inv[...]
        z[:, :, :, lanes] = value
        sums[...] += value * value

    loop(0, BLOCKS, centre)
    var = jnp.sum(sums[...], axis=3, keepdims=True) * (1.0 / CHANNELS)
    inv[...] = jnp.broadcast_to(lax.rsqrt(var + EPSILON), sums.shape)

    def norm(block):
        lanes = lanes_of(block)
        value = z[:, :, :, lanes] * inv[...]
        z[:, :, :, lanes] = value
        zs = jnp.sum(jnp.sum(value, axis=1), axis=1)
        zsum[:, lanes] = zs
        gain = full[pl.ds(BLOCK_ROW, 1), lanes]
        img = jnp.sum(isum[:, :, lanes], axis=1)
        pooled[:, lanes] = (img + zs * gain) * (1.0 / (MAP_SIDE * MAP_SIDE))

    loop(0, BLOCKS, norm)
    value = pooled[...]
    centred = value - jnp.mean(value, axis=1, keepdims=True)
    inverse = lax.rsqrt(jnp.mean(centred * centred, axis=1, keepdims=True) + EPSILON)
    return centred * inverse, inverse


def backward_block(block, images, z, inv, full, dh, dn, sums, mean1, grads, gimg):
    margin = KERNEL // 2
    lanes = lanes_of(block)
    maps, pixels, acc = [], [], []
    bias = None
    for b in range(IMGS):
        row = jnp.broadcast_to(dn[pl.ds(b, 1), lanes], (MAP_SIDE, 128)) - jnp.broadcast_to(
            mean1[pl.ds(b, 1), :], (MAP_SIDE, 128)
        )
        hidden = jnp.broadcast_to(dh[pl.ds(b, 1), lanes], (MAP_SIDE, 128))
        for i in range(MAP_SIDE):
            value = inv[b, i] * (row - z[b, i, :, lanes] * sums[b, i])
            maps.append(value)
            bias = value if bias is None else bias + value
            pixels.append(images[b, i, :, lanes].astype(F32))
            acc.append(hidden)
    grads[pl.ds(BIAS_ROW, 1), lanes] = jnp.sum(bias, axis=0, keepdims=True)
    for s in range(KERNEL):
        grad = [None] * KERNEL
        for b in range(IMGS):
            own = range(b * MAP_SIDE, (b + 1) * MAP_SIDE)
            cols = [shifted(maps[k], s - margin) for k in own]
            for r in range(KERNEL):
                tap = jnp.broadcast_to(full[pl.ds(r * KERNEL + s, 1), lanes], (MAP_SIDE, 128))
                for i in range(MAP_SIDE):
                    if 0 <= i - r + margin < MAP_SIDE:
                        col = cols[i - r + margin]
                        k = own[i]
                        acc[k] = acc[k] + col * tap
                        term = col * pixels[k]
                        grad[r] = term if grad[r] is None else grad[r] + term
        for r in range(KERNEL):
            grads[pl.ds(r * KERNEL + s, 1), lanes] = jnp.sum(grad[r], axis=0, keepdims=True)
    for b in range(IMGS):
        for i in range(MAP_SIDE):
            gimg[b, i, :, lanes] = acc[b * MAP_SIDE + i].astype(BF16)


def step_kernel(
    images_hbm, w_hbm, bias_hbm, gain_hbm, head_hbm, proj_hbm, text_hbm,
    gimg, taps_out, bias_out, block_out, head_out, loss_out, proj_out, gtext_out,
    images, w_in, bias_in, gain_in, head_in, proj_in, text_in,
    pack, held, full, z, inv, zsum, sums, isum, pooled,
    normed_s, normed_r, part_s, part_r, img_s, img_r, row_s, row_r, dimg_s, dimg_r,
    demb_s, demb_r, dn_s, dn_r, text_s, text_r, col_s, col_r, dcap_s, dcap_r,
    dnormed, projgrad, grads, dh, dn, mean1, blocks_s, mate_r, chip_s, chip_r,
    small, proj_r, small_r, proj_mine, small_mine, proj_all, small_all,
    load_sem, fs, fr, ds, dr, ps, pr, ss, sr, gs, gr, hs, hr, near_s, near_r, far_s, far_r,
):
    me_f, me_d = lax.axis_index("fsdp"), lax.axis_index("dp")
    my_pair, core = lax.div(me_f, 2), lax.rem(me_f, 2)
    mate = 2 * my_pair + 1 - core
    greet(me_f, me_d)
    loads = [
        pltpu.make_async_copy(src, dst, load_sem.at[n])
        for n, (src, dst) in enumerate(
            (
                (w_hbm, w_in), (bias_hbm, bias_in), (gain_hbm, gain_in), (text_hbm, text_in),
                (images_hbm, images), (head_hbm, head_in), (proj_hbm, proj_in),
            )
        )
    ]
    for load in loads:
        load.start()

    def fex(n, source, dst):
        return Exchange("fsdp", N_FSDP, me_f, source, dst, fs.at[n], fr.at[n])

    def dex(n, source, dst):
        return Exchange("dp", N_DP, me_d, source, dst, ds.at[n], dr.at[n])

    sums[...] = jnp.zeros_like(sums)
    for load in loads[:4]:
        load.wait()
    rows = dense(jnp.concatenate([w_in[...], bias_in[...], gain_in[...]], axis=0))
    pack[...] = rows
    held[me_f] = rows
    text = text_in[...].astype(F32)
    text_scale = lax.rsqrt(jnp.sum(text * text, axis=1, keepdims=True) + EPSILON)
    text_f = text * text_scale
    text_unit = text_f.astype(BF16)
    text_s[...] = text_unit
    text_r[me_d] = text_unit
    greeted()

    def near_copy(p, block, dst):
        return copy_to("fsdp", mate, block, dst, near_s, near_r.at[p])

    def far_copy(t, n, block, dst):
        q = lax.rem(my_pair + t, PAIRS)
        return copy_to("fsdp", 2 * q + core, block, dst, far_s.at[n], far_r.at[n, my_pair])

    near_copy(my_pair, pack, held.at[me_f]).start()
    loop(1, PAIRS, lambda t: far_copy(t, 0, pack, held.at[me_f]).start())
    x_text = dex(0, lambda peer: text_s, text_r)
    x_text.start()
    for load in loads[4:]:
        load.wait()

    def hand_on(t):
        p = lax.rem(my_pair - t + PAIRS, PAIRS)
        block = held.at[2 * p + core]
        copy_to("fsdp", 2 * p + core, block, block, far_s.at[0], far_r.at[0, p]).wait_recv()
        near_copy(p, block, block).start()

    def forward_pair(t):
        p = lax.rem(my_pair - t + PAIRS, PAIRS)
        block = held.at[2 * p + 1 - core]
        near_copy(p, block, block).wait_recv()
        left, right = held[2 * p], held[2 * p + 1]
        full[:DENSE, pair_lanes(p)] = jnp.concatenate([left[:, :SHARD], right[:, :SHARD]], axis=1)
        full[DENSE:TAKEN, pair_lanes(p)] = jnp.concatenate([rest_of(left), rest_of(right)], axis=1)
        loop(0, 3, lambda k: forward_block(3 * p + k, images, full, z, sums, isum))

        @pl.when(t == 0)
        def _():
            hand_on(1)

        @pl.when(t + 2 < PAIRS)
        def _():
            hand_on(t + 2)

    loop(0, PAIRS, forward_pair)
    pool_normed, pool_inverse = forward_norm(full, z, inv, zsum, sums, isum, pooled)

    for p in range(PAIRS):
        value = pool_normed[:, 384 * p : 384 * (p + 1)]
        normed_s[2 * p] = value[:, :SHARD]
        normed_s[2 * p + 1] = value[:, SHARD:]
    pooled[...] = pool_normed
    normed_r[me_f] = normed_s[me_f]
    x_norm = fex(0, lambda peer: normed_s.at[peer], normed_r)
    x_norm.start()
    x_text.wait_recv()
    text_cols = stack(text_r, N_DP)
    x_norm.wait_recv()
    normed = stack(normed_r, N_FSDP)
    head = head_in[...]
    query = (normed * head).astype(BF16)
    part = jnp.dot(query, proj_in[...], preferred_element_type=F32)
    spread(part_s, part)
    part_r[me_f] = part_s[me_f]
    x_part = fex(1, lambda peer: part_s.at[peer], part_r)
    x_part.start()
    x_part.wait_recv()
    embedding = total(part_r, N_FSDP)
    image_scale = lax.rsqrt(jnp.sum(embedding * embedding, axis=1, keepdims=True) + EPSILON)
    image_f = embedding * image_scale
    image_unit = image_f.astype(BF16)
    img_s[...] = image_unit
    img_r[me_f] = image_unit
    x_img = fex(2, lambda peer: img_s, img_r)
    x_img.start()
    diagonal = LOGIT_SCALE * jnp.sum(image_unit.astype(F32) * text_unit.astype(F32))

    n_row, n_col = N_FSDP * IMGS, N_DP * IMGS
    eye = (
        lax.broadcasted_iota(jnp.int32, (n_row, 128), 0)
        == lax.broadcasted_iota(jnp.int32, (n_row, 128), 1)
    )
    x_img.wait_recv()
    image_rows = stack(img_r, N_FSDP)
    logits = LOGIT_SCALE * contract(image_rows, text_cols, 1, 1)
    exps = jnp.exp(logits)
    col_part = jnp.sum(exps, axis=0, keepdims=True)
    col_flat = jnp.concatenate([col_part, jnp.zeros((1, 128 - n_col), F32)], axis=1)
    col_s[...] = col_flat
    col_r[me_d] = col_flat
    x_col = dex(1, lambda peer: col_s, col_r)
    x_col.start()
    row_part = jnp.sum(exps, axis=1, keepdims=True)
    row_flat = jnp.sum(jnp.where(eye, row_part, 0.0), axis=0, keepdims=True)
    row_s[...] = row_flat
    row_r[me_f] = row_flat
    x_row = fex(3, lambda peer: row_s, row_r)
    x_row.start()
    x_row.wait_recv()
    row_sum = total(row_r, N_FSDP)
    row_lse = jnp.log(jnp.sum(jnp.where(eye, row_sum, 0.0), axis=1, keepdims=True))
    row_term = jnp.exp(logits - row_lse)
    at_row = lax.broadcasted_iota(jnp.int32, (n_row, n_col), 0)
    at_col = lax.broadcasted_iota(jnp.int32, (n_row, n_col), 1)
    pair = jnp.where(
        (at_row - IMGS * me_f == at_col - IMGS * me_d)
        & (at_row >= IMGS * me_f)
        & (at_row < IMGS * me_f + IMGS),
        2.0,
        0.0,
    )
    x_col.wait_recv()
    col_lse = jnp.log(total(col_r, N_DP)[:, :n_col])
    weights = (row_term + jnp.exp(logits - col_lse) - pair).astype(BF16)
    dimg = jnp.dot(weights, text_cols, preferred_element_type=F32)
    spread(dimg_s, dimg)
    dimg_r[me_f] = dimg_s[me_f]
    x_dimg = fex(4, lambda peer: dimg_s.at[peer], dimg_r)
    x_dimg.start()
    dcap = contract(weights, image_rows, 0, 0)
    spread(dcap_s, dcap)
    dcap_r[me_d] = dcap_s[me_d]
    x_dcap = dex(2, lambda peer: dcap_s.at[peer], dcap_r)
    x_dcap.start()
    loss_part = (
        jnp.sum(row_lse) * (1.0 / N_FSDP) + jnp.sum(col_lse) * (1.0 / N_DP) - 2.0 * diagonal
    )
    x_dimg.wait_recv()
    d_image = 7.0 * total(dimg_r, N_FSDP)
    d_embedding = (
        image_scale * (d_image - image_f * jnp.sum(image_f * d_image, axis=1, keepdims=True))
    ).astype(BF16)
    demb_s[...] = d_embedding
    demb_r[me_f] = d_embedding
    x_demb = fex(5, lambda peer: demb_s, demb_r)
    x_demb.start()
    x_demb.wait_recv()
    demb = stack(demb_r, N_FSDP)
    d_query = contract(demb, proj_in[...], 1, 1)
    spread(dn_s, d_query * head)
    dn_r[me_f] = dn_s[me_f]
    x_dn = fex(6, lambda peer: dn_s.at[peer], dn_r)
    x_dn.start()
    head_grad = jnp.sum(d_query * normed, axis=0, keepdims=True)
    projgrad[...] = contract(query, demb, 0, 0)

    first = PROJ_OWNERS
    last = PROJ_OWNERS + SMALL_OWNERS

    def proj_rows(k):
        return pl.ds(pl.multiple_of(k * 8, 8), 8)

    def small_rows(k):
        return pl.ds(pl.multiple_of((k - first) * 8, 8), 8)

    def peers(act):
        far_first(N_DP, 12, lambda offset: act(offset, lax.rem(me_d + offset, N_DP)))

    def proj_copy(t, peer, to):
        return copy_to("dp", peer, projgrad.at[proj_rows(to)], proj_r.at[me_d], ps, pr)

    def small_copy(t, peer, to):
        return copy_to("dp", peer, small.at[small_rows(to)], small_r.at[me_d], ss, sr)

    def start_proj(t, peer):
        @pl.when(peer < first)
        def _():
            proj_copy(t, peer, peer).start()

    peers(start_proj)

    x_dn.wait_recv()

    def write(p, value):
        dnormed[:, 384 * p : 384 * (p + 1)] = value

    join_pairs(lambda k: dn_r[k], write)

    normed = pooled[...]
    d_normed = dnormed[...]
    d_pooled = pool_inverse * (
        d_normed
        - jnp.mean(d_normed, axis=1, keepdims=True)
        - normed * jnp.mean(d_normed * normed, axis=1, keepdims=True)
    )
    d_hidden = d_pooled * (1.0 / (MAP_SIDE * MAP_SIDE))
    dh[...] = d_hidden
    d_norm = d_hidden * full[BLOCK_ROW : BLOCK_ROW + 1, :]
    dn[...] = d_norm
    grads[ROWS - 8 :, :] = jnp.zeros((8, CHANNELS), F32)
    grads[BLOCK_ROW : BLOCK_ROW + 1, :] = jnp.sum(d_hidden * zsum[...], axis=0, keepdims=True)
    grads[LOSS_ROW : LOSS_ROW + 1, :] = jnp.full(
        (1, CHANNELS), loss_part * (0.5 / (N_DP * N_FSDP * IMGS)), F32
    )
    mean1[...] = jnp.broadcast_to(jnp.mean(d_norm, axis=1, keepdims=True), mean1.shape)
    sums[...] = jnp.zeros_like(sums)

    def project(block):
        lanes = lanes_of(block)
        for b in range(IMGS):
            row = jnp.broadcast_to(dn[pl.ds(b, 1), lanes], (MAP_SIDE, 128))
            for i in range(MAP_SIDE):
                sums[b, i] += row * z[b, i, :, lanes]

    loop(0, BLOCKS, project)
    mean2 = jnp.sum(sums[...], axis=3, keepdims=True) * (1.0 / CHANNELS)
    sums[...] = jnp.broadcast_to(mean2, sums.shape)

    owns_proj = me_d < first

    def dp_wait(like, blocks, send_sem, recv_sem):
        wait_blocks("dp", N_DP, me_d, like, blocks, send_sem, recv_sem)

    my_z, my_x = lax.div(me_d, 2), lax.rem(me_d, 2)
    n_z = N_DP // 2
    z_owners = PROJ_OWNERS // 2

    def proj_start():
        def body(offset):
            to = 2 * lax.rem(my_z + offset, n_z) + my_x
            copy_to("dp", to, proj_mine, proj_all.at[my_x, my_z], gs.at[0], gr.at[0]).start()

        far_first(n_z, n_z // 2 - 2, body)

    def proj_window(x, blocks):
        return proj_all.at[x, pl.ds(0, blocks)]

    def proj_wait(x, blocks, send_sem, recv_sem):
        window = proj_window(x, blocks)
        sem = recv_sem if send_sem is None else send_sem
        copy = copy_to("dp", me_d + 1 - 2 * my_x, window, window, sem, sem)
        if send_sem is None:
            copy.wait_recv()
        else:
            copy.wait_send()

    def proj_hand_on():
        window = proj_window(my_x, z_owners)
        return copy_to("dp", me_d + 1 - 2 * my_x, window, window, gs.at[2], gr.at[2])

    def sum_proj():
        proj_r[me_d] = projgrad[proj_rows(me_d), :]
        dp_wait(proj_r, N_DP - 1, None, pr)
        out = total(proj_r, N_DP).astype(BF16)
        proj_mine[...] = out
        proj_all[my_x, my_z] = out
        proj_start()

    def mate_copy(p):
        return copy_to(
            "fsdp", mate, blocks_s.at[2 * p + 1 - core], mate_r.at[p], hs, hr.at[p]
        )

    def chip_sum(p):
        copy_to("fsdp", mate, mate_r.at[p], mate_r.at[p], hs, hr.at[p]).wait_recv()
        return blocks_s[2 * p + core] + mate_r[p]

    def backward_order(t):
        y, x = lax.div(my_pair, 2), lax.rem(my_pair, 2)
        return 2 * lax.rem(y + 1 + lax.div(t - 1, 2), PAIRS // 2) + lax.rem(x + t, 2)

    def send_chip(t):
        p = backward_order(t)
        chip_s[p] = chip_sum(p)
        copy_to(
            "fsdp", 2 * p + core, chip_s.at[p], chip_r.at[my_pair], far_s.at[1], far_r.at[1, my_pair]
        ).start()

    def backward_pair(t):
        p = backward_order(t)

        def piece(k):
            backward_block(3 * p + k, images, z, inv, full, dh, dn, sums, mean1, grads, gimg)

            @pl.when((k == 0) & (t > 1))
            def _():
                send_chip(t - 1)

        loop(0, 3, piece)
        value = grads[:, pair_lanes(p)]
        blocks_s[2 * p] = value[:, :SHARD]
        blocks_s[2 * p + 1] = value[:, SHARD:]
        mate_copy(p).start()

    loop(1, PAIRS + 1, backward_pair)
    chip_r[my_pair] = chip_sum(my_pair)

    def chip_wait(t):
        p = lax.rem(my_pair + t, PAIRS)
        copy_to(
            "fsdp", 2 * p + core, chip_r.at[p], chip_r.at[p], far_s.at[1], far_r.at[1, p]
        ).wait_recv()

    loop(1, PAIRS, chip_wait)
    small[...] = total(chip_r, PAIRS)
    small[HEAD_ROW : HEAD_ROW + 1, :] = head_grad

    def start_small(t, peer):
        @pl.when((peer >= first) & (peer < last))
        def _():
            small_copy(t, peer, peer).start()

    peers(start_small)

    def small_all_copy(peer):
        return copy_to("dp", peer, small_mine, small_all.at[me_d - first], gs.at[1], gr.at[1])

    @pl.when(owns_proj)
    def _():
        sum_proj()

    owns_small = (me_d >= first) & (me_d < last)

    @pl.when(owns_small)
    def _():
        small_r[me_d] = small[small_rows(me_d), :]
        dp_wait(small_r, N_DP - 1, None, sr)
        out = total(small_r, N_DP)
        small_mine[...] = out
        small_all[me_d - first] = out
        peers(lambda t, peer: small_all_copy(peer).start())

    x_dcap.wait_recv()
    d_caption = 7.0 * total(dcap_r, N_DP)
    gtext_out[...] = text_scale * (
        d_caption - text_f * jnp.sum(text_f * d_caption, axis=1, keepdims=True)
    )

    for ex in (x_text, x_norm, x_part, x_img, x_col, x_row, x_dimg, x_dcap, x_demb, x_dn):
        ex.wait_send()
    wait_blocks("fsdp", N_FSDP, me_f, held, PAIRS, near_s, None)
    wait_blocks("fsdp", N_FSDP, me_f, held, PAIRS - 1, far_s.at[0], None)
    wait_blocks("fsdp", N_FSDP, me_f, mate_r, PAIRS, hs, None)
    wait_blocks("fsdp", N_FSDP, me_f, chip_r, PAIRS - 1, far_s.at[1], None)

    @pl.when(owns_proj)
    def _():
        dp_wait(proj_r, PROJ_OWNERS - 1, ps, None)
        proj_wait(my_x, z_owners - 1, None, gr.at[0])

    @pl.when(me_d >= first)
    def _():
        dp_wait(proj_r, PROJ_OWNERS, ps, None)
        proj_wait(my_x, z_owners, None, gr.at[0])

    handed = proj_hand_on()
    handed.start()

    @pl.when(owns_small)
    def _():
        dp_wait(small_r, SMALL_OWNERS - 1, ss, None)
        dp_wait(small_all, SMALL_OWNERS - 1, None, gr.at[1])
        dp_wait(small_r, N_DP - 1, gs.at[1], None)

    @pl.when((me_d < first) | (me_d >= last))
    def _():
        dp_wait(small_r, SMALL_OWNERS, ss, None)
        dp_wait(small_all, SMALL_OWNERS, None, gr.at[1])

    for k in range(BIAS_ROW // 8):
        taps_out[8 * k : 8 * (k + 1), :] = small_all[k]
    rest = small_all[BIAS_ROW // 8]
    taps_out[BIAS_ROW - 1 :, :] = rest[:1]
    bias_out[...] = rest[BIAS_ROW - 48 : BIAS_ROW - 47]
    block_out[...] = rest[BLOCK_ROW - 48 : BLOCK_ROW - 47]
    head_out[...] = rest[HEAD_ROW - 48 : HEAD_ROW - 47]
    loss_out[...] = rest[LOSS_ROW - 48 : LOSS_ROW - 47, :128]

    @pl.when(owns_proj)
    def _():
        proj_wait(0, n_z - 1, gs.at[0], None)

    proj_wait(1 - my_x, z_owners, None, gr.at[2])
    for k in range(PROJ_OWNERS):
        proj_out[8 * k : 8 * (k + 1), :] = proj_all[k % 2, k // 2].astype(F32)
    handed.wait_send()


def store_kernel(*refs):
    count = (len(refs) - 1) // 2
    copies = [
        pltpu.make_async_copy(refs[n], refs[count + n], refs[-1].at[n]) for n in range(count)
    ]
    for copy in copies:
        copy.start()
    for copy in copies:
        copy.wait()


def dma(*shape):
    return pltpu.SemaphoreType.DMA(shape)


def local(images, dw_weight, dw_bias, block_gain, head_gain, projection, text):
    V = pltpu.VMEM
    maps = (IMGS, MAP_SIDE, MAP_SIDE, CHANNELS)
    lanes = (IMGS, MAP_SIDE, MAP_SIDE, 128)
    wide = (IMGS, CHANNELS)
    two = (IMGS, EMBED)

    def f_blocks(shape, kind):
        return V((N_FSDP,) + shape, kind)

    def d_blocks(shape, kind):
        return V((N_DP,) + shape, kind)

    inputs = (images, dw_weight, dw_bias[None], block_gain[None], head_gain[None], projection, text)
    inputs = [pltpu.with_memory_space_constraint(value, pltpu.HBM) for value in inputs]
    row = (1, SHARD)
    outs = [
        jax.ShapeDtypeStruct(shape, kind)
        for shape, kind in (
            (maps, BF16), ((KERNEL * KERNEL, SHARD), F32), (row, F32), (row, F32), (row, F32),
            ((1, 128), F32), ((SHARD, EMBED), F32), (two, F32),
        )
    ]
    results = pl.pallas_call(
        step_kernel,
        out_shape=outs,
        in_specs=[pl.BlockSpec(memory_space=pltpu.HBM)] * len(inputs),
        out_specs=[VMEM_SPEC] * len(outs),
        scratch_shapes=[
            V(maps, BF16), V((KERNEL * KERNEL, SHARD), F32), V((1, SHARD), F32), V((1, SHARD), F32),
            V((1, SHARD), F32), V((SHARD, EMBED), BF16), V(two, BF16),
            V((DENSE, 256), F32), f_blocks((DENSE, 256), F32), V((ROWS, CHANNELS), F32),
            V(maps, F32), V(lanes, F32), V(wide, F32), V(lanes, F32),
            V((IMGS, MAP_SIDE, CHANNELS), F32), V(wide, F32),
            f_blocks((IMGS, SHARD), F32), f_blocks((IMGS, SHARD), F32),
            f_blocks(two, F32), f_blocks(two, F32),
            V(two, BF16), f_blocks(two, BF16),
            V((1, 128), F32), f_blocks((1, 128), F32),
            f_blocks(two, F32), f_blocks(two, F32),
            V(two, BF16), f_blocks(two, BF16),
            f_blocks((IMGS, SHARD), F32), f_blocks((IMGS, SHARD), F32),
            V(two, BF16), d_blocks(two, BF16),
            V((1, 128), F32), d_blocks((1, 128), F32),
            d_blocks(two, F32), d_blocks(two, F32),
            V(wide, F32), V((SHARD, EMBED), F32), V((ROWS, CHANNELS), F32), V(wide, F32),
            V(wide, F32), V((IMGS, 128), F32), f_blocks((ROWS, SHARD), F32),
            V((PAIRS, ROWS, SHARD), F32), V((PAIRS, ROWS, SHARD), F32), V((PAIRS, ROWS, SHARD), F32),
            V((ROWS, SHARD), F32), d_blocks((8, EMBED), F32), d_blocks((8, SHARD), F32),
            V((8, EMBED), BF16), V((8, SHARD), F32),
            V((2, N_DP // 2, 8, EMBED), BF16), V((SMALL_OWNERS, 8, SHARD), F32),
            dma(7), dma(7), dma(7), dma(3), dma(3), dma(), dma(), dma(), dma(), dma(3), dma(3),
            dma(), dma(PAIRS), dma(), dma(PAIRS), dma(2), dma(2, PAIRS),
        ],
        compiler_params=pltpu.CompilerParams(
            vmem_limit_bytes=48 * 1024 * 1024, collective_id=0, has_side_effects=True
        ),
    )(*inputs)
    grad_images, taps, bias, block, head, loss, sum_proj, grad_text = pl.pallas_call(
        store_kernel,
        out_shape=outs,
        in_specs=[VMEM_SPEC] * len(outs),
        out_specs=[pl.BlockSpec(memory_space=pltpu.HBM)] * len(outs),
        scratch_shapes=[dma(len(outs))],
        compiler_params=pltpu.CompilerParams(vmem_limit_bytes=1024 * 1024),
    )(*results)
    return (loss[0, 0], grad_images, taps, bias[0], block[0], head[0], sum_proj, grad_text)


def solution(mesh):
    return jax.shard_map(
        local,
        mesh=mesh,
        in_specs=(
            P(("dp", "fsdp"), None, None, None),
            P(None, "fsdp"),
            P("fsdp"),
            P("fsdp"),
            P("fsdp"),
            P("fsdp", None),
            P(("dp", "fsdp"), None),
        ),
        out_specs=(
            P(),
            P(("dp", "fsdp"), None, None, None),
            P(None, "fsdp"),
            P("fsdp"),
            P("fsdp"),
            P("fsdp"),
            P("fsdp", None),
            P(("dp", "fsdp"), None),
        ),
        check_vma=False,
    )
```
